256 devices in a mesh: geo: 4 (over y), region: 16 (over z, core), sub: 4 (over x).
Axes of the slice: x: 4, y: 4, z: 8, core: 2. Of those that a mesh axis runs over, the one named last changes fastest.
Arguments:
- features: bfloat16 [4, 32, 131072], P('geo', None, ('region', 'sub')), may hold values from -6 to 6
- lap_tiles: bfloat16 [4, 1024, 4, 128, 128], P('geo', ('region', 'sub')), may hold values from -0.25 to 0.25
- tile_cols: int32 [4, 1024, 4], P('geo', ('region', 'sub')), may hold values from 0 to 17
- coarse_owner: int32 [4, 131072, 1], P('geo', ('region', 'sub')), may hold values from 0 to 63; in each aligned block of 2048 rows (0 to 2047, 2048 to 4095, ..., all dimensions but the last counted through in order) at most 128 rows name the same one
- coarse_slot: int32 [4, 131072], P('geo', ('region', 'sub')), may hold values from 0 to 511
- pool_weight: float32 [4, 131072], P('geo', ('region', 'sub')), may hold values from 0.25 to 1
- weight_in: bfloat16 [3, 32, 32], replicated, may hold values from -0.625 to 0.625
- weight_mid: bfloat16 [32, 32], replicated, may hold values from -1 to 1
- weight_out: bfloat16 [3, 32, 32], replicated, may hold values from -0.625 to 0.625
- biases: float32 [2, 32], replicated, may hold values from -3 to 3
- out_grad: bfloat16 [4, 32, 131072], P('geo', None, ('region', 'sub')), may hold values from -6 to 6
Outputs:
- result: bfloat16 [4, 32, 131072], P('geo', None, ('region', 'sub'))
- input_grad: bfloat16 [4, 32, 131072], P('geo', None, ('region', 'sub'))
- weight_grads: float32 [7, 32, 32], replicated
- bias_grads: float32 [2, 32], replicated
The draws below stay inside these ranges and needn't reach their ends.
Inputs may be any that keep to these rules, and one draw needn't show every extreme that they name: `coarse_owner`: among the 2048 fine vertices of one device (aligned blocks along the vertices, geometries in order) no owner is named more than 128 times, and in every draw some owner is named exactly 128 times. `tile_cols`: entry 0 reads the last tile of the device before, 1 to 16 the device's own tiles, 17 the first tile of the device after.
All inputs are finite; a program needn't handle non-finite values.
Results may differ from the reference program's by a relative error of at most 0.02.
Values may be sent and summed in bfloat16 or wider, within the bound.
No kernel may reach another device: no remote copies, remote signals or barrier semaphores. Data moves between devices by JAX's collectives and lax.ppermute only.
A program may use at most 64 MiB of HBM per device.

```python
import math
import jax
import jax.numpy as jnp
import numpy as np
from jax import lax

C = 32
TB = 128
NNZ = 4
KT = 16
GEOS = 4
FDEV = 2048
NDEST = 64
CAP = 128
CDEV = 512
NF = 131072
NTILES = 1024
NC = 32768


def touch_ends(array, rng, smallest, largest):
    longest = array.shape.index(max(array.shape))
    spots = []
    for shift in (0, 1):
        where = [jax.random.randint(jax.random.fold_in(rng, axis), (), 0, length) for axis, length in enumerate(array.shape)]
        where[longest] = (where[longest] + shift) % array.shape[longest]
        spots.append(tuple(where))
    return array.at[spots[0]].set(smallest).at[spots[1]].set(largest)


def steps_of(rng, shape, cuts, least, high):
    gain, own = 1.0, jax.random.fold_in(rng, 6)
    for position, shards_of in cuts:
        heights = jnp.exp(jax.random.uniform(jax.random.fold_in(own, position), (shards_of,), jnp.float32, least / len(cuts), high / len(cuts)))
        gain = gain * jnp.repeat(heights, shape[position] // shards_of).reshape([-1 if axis == position else 1 for axis in range(len(shape))])
    return gain


def routed_block(stream_key, own, number, rows, number_of, top, most, lean):
    order = jax.random.permutation(stream_key, number_of)
    heavy_load, ordinary = load_shares(number_of, rows * top, most, lean, True), load_shares(number_of, rows * top, most, lean, False)
    places = jnp.arange(number_of)

    def named(lengths, rotation):
        used = int((lengths > 0).sum())
        fixed = max(1, used // 4)
        moved = fixed + (places - fixed + rotation * (used - fixed)) % max(1, number_of - fixed)
        return jnp.zeros((number_of,), jnp.int32).at[order[jnp.where(places < fixed, places, moved)]].set(jnp.asarray(lengths, jnp.int32))

    lengths = jnp.where(number % 4 == 0, named(heavy_load, number // 4), named(ordinary, number - number // 4 - 1))
    mixed = jax.random.permutation(jax.random.fold_in(own, 3), number_of)
    giver, sink = mixed[0:number_of // 2 * 2:2], mixed[1:number_of // 2 * 2:2]
    margin = jnp.minimum(lengths[giver] - 1, most - lengths[sink]) // 2
    margin = jnp.where((giver == order[0]) | (sink == order[0]) | (lengths[sink] == 0), 0, jnp.maximum(margin, 0))
    moved = jax.random.randint(jax.random.fold_in(own, 4), (number_of // 2,), 0, 1 << 20) % (margin + 1)
    lengths = lengths.at[giver].add(-moved).at[sink].add(moved)
    items = jnp.searchsorted(jnp.cumsum(lengths), jnp.arange(rows * top), side="right").astype(jnp.int32)
    listing = items.reshape(top, rows).T
    listing = listing[jax.random.permutation(jax.random.fold_in(own, 1), rows)]
    rotation = jax.random.randint(jax.random.fold_in(own, 2), (rows, 1), 0, top)
    return jnp.take_along_axis(listing, (jnp.arange(top)[None, :] + rotation) % top, axis=1)


def load_shares(count, total, limit, skew, full):
    loads = [(1 << 20) // math.isqrt(grade ** skew) + 1 for grade in range(1, count + 1)]
    largest = limit if full else min(limit, max(-(-total // count), total * loads[0] // sum(loads)))
    least = 1 if total - largest >= count - 1 else 0
    holding, spare = [largest] + [least] * (count - 1), total - largest - least * (count - 1)
    while spare > 0:
        movable = [i for i in range(1, count) if holding[i] < largest] or [i for i in range(1, count) if holding[i] < limit]
        pool, left = sum([loads[i] for i in movable]), spare
        for i in movable:
            more = min(limit - holding[i], max(1, left * loads[i] // pool), spare)
            holding[i] = holding[i] + more
            spare = spare - more
    return np.array(holding)


def centred(own_key, shape, spread, reach, split=(), held_as=jnp.bfloat16):
    array = spread * jax.random.normal(own_key, shape, jnp.float32)
    if split:
        array = array * steps_of(own_key, shape, split, -0.22, 0.18)
    return jnp.clip(array, -reach, reach).astype(held_as)


def setup_inputs(seed: int = 0) -> dict:
    arg_keys = jax.random.split(jax.random.key(seed), 12)
    features = centred(arg_keys[0], (GEOS, C, NF), 1.0, 6.0, ((0, 4), (2, 64)))
    lap_tiles = centred(arg_keys[1], (GEOS, NTILES, NNZ, TB, TB), (NNZ * TB) ** -0.5, 0.25, ((0, 4), (1, 64)))
    tile_cols = touch_ends(jax.random.randint(arg_keys[2], (GEOS, NTILES, NNZ), 0, KT + 2), jax.random.fold_in(arg_keys[2], 1), 0, (KT + 2) - 1).astype(jnp.int32)
    coarse_owner_keys = jax.random.split(jax.random.fold_in(arg_keys[3], 1), GEOS * NF // FDEV)
    coarse_owner_turns = jax.random.permutation(jax.random.fold_in(arg_keys[3], 3), GEOS * NF // FDEV)
    coarse_owner = jax.vmap(lambda own, number: routed_block(jax.random.fold_in(arg_keys[3], 2), own, number, FDEV, NDEST, 1, CAP, 2))(coarse_owner_keys, coarse_owner_turns).reshape((GEOS, NF, 1))
    coarse_slot = touch_ends(jax.random.randint(arg_keys[4], (GEOS, NF), 0, CDEV), jax.random.fold_in(arg_keys[4], 1), 0, CDEV - 1).astype(jnp.int32)
    pool_weight = jnp.clip(jnp.exp(math.log(1.0) - 1.3862944 * jax.random.uniform(arg_keys[5], (GEOS, NF), jnp.float32) ** steps_of(arg_keys[5], (GEOS, NF), ((0, 4), (1, 64)), -0.2, 0.2)), 0.25, 1.0)
    weight_in = centred(arg_keys[6], (3, C, C), (3 * C) ** -0.5, 0.625)
    weight_mid = centred(arg_keys[7], (C, C), C ** -0.5, 1.0)
    weight_out = centred(arg_keys[8], (3, C, C), (3 * C) ** -0.5, 0.625)
    biases = centred(arg_keys[9], (2, C), 0.5, 3.0, (), jnp.float32)
    out_grad = centred(arg_keys[10], (GEOS, C, NF), 1.0, 6.0, ((0, 4), (2, 64)))
    return {"features": features, "lap_tiles": lap_tiles, "tile_cols": tile_cols, "coarse_owner": coarse_owner, "coarse_slot": coarse_slot, "pool_weight": pool_weight, "weight_in": weight_in, "weight_mid": weight_mid, "weight_out": weight_out, "biases": biases, "out_grad": out_grad}


def apply_operator(field, tiles, columns):
    padded = jnp.pad(field, ((0, 0), (TB, TB))).reshape(C, NTILES + 2, TB)

    def per_device(device):
        local_tiles = lax.dynamic_slice_in_dim(tiles, device * KT, KT, 0).astype(jnp.float32)
        local_cols = lax.dynamic_slice_in_dim(columns, device * KT, KT, 0) + device * KT
        picked = padded[:, local_cols].astype(jnp.float32)
        return jnp.einsum('cknt,kntu->cku', picked, local_tiles)
    stacked = lax.map(per_device, jnp.arange(NDEST, dtype=jnp.int32))
    return jnp.transpose(stacked, (1, 0, 2, 3)).reshape(C, NF)

def apply_transpose(grad, tiles, columns):
    blocks = grad.reshape(C, NTILES, TB)

    def per_device(total, device):
        local_tiles = lax.dynamic_slice_in_dim(tiles, device * KT, KT, 0).astype(jnp.float32)
        local_cols = lax.dynamic_slice_in_dim(columns, device * KT, KT, 0) + device * KT
        local_grad = lax.dynamic_slice_in_dim(blocks, device * KT, KT, 1).astype(jnp.float32)
        contrib = jnp.einsum('cku,kntu->cknt', local_grad, local_tiles)
        return (total.at[:, local_cols].add(contrib), None)
    total, unused = lax.scan(per_device, jnp.zeros((C, NTILES + 2, TB), jnp.float32), jnp.arange(NDEST, dtype=jnp.int32))
    return total[:, 1:-1].reshape(C, NF)

def mixdot(weight, field):
    return jnp.dot(weight, field, preferred_element_type=jnp.float32)

def cheb_forward(field, weights, tiles, columns):
    first = apply_operator(field, tiles, columns).astype(jnp.bfloat16)
    second = (2.0 * apply_operator(first, tiles, columns) - field.astype(jnp.float32)).astype(jnp.bfloat16)
    output = mixdot(weights[0], field) + mixdot(weights[1], first) + mixdot(weights[2], second)
    return (output, (field, first, second))

def cheb_backward(grad, weights, tiles, columns):
    second = mixdot(weights[2].T, grad).astype(jnp.bfloat16)
    first = (mixdot(weights[1].T, grad) + 2.0 * apply_transpose(second, tiles, columns)).astype(jnp.bfloat16)
    return mixdot(weights[0].T, grad) - second.astype(jnp.float32) + apply_transpose(first, tiles, columns)

def silu_slope(value):
    sig = jax.nn.sigmoid(value)
    return sig * (1.0 + value * (1.0 - sig))

def outer_sum(left, right):
    return jnp.dot(left, right.T, preferred_element_type=jnp.float32)

def pool_sum(message, parent):
    return jax.ops.segment_sum(message.astype(jnp.float32).T, parent, num_segments=NC).T

def replica(inputs):
    features, tiles, columns, owners, slots, pool_weight, weight_in, weight_mid, weight_out, biases, out_grad = inputs
    parent = owners[:, 0] * CDEV + slots
    weight_row = pool_weight[None, :]
    pre_sum, terms_in = cheb_forward(features, weight_in, tiles, columns)
    pre_in = pre_sum + biases[0][:, None]
    hidden = jax.nn.silu(pre_in).astype(jnp.bfloat16)
    message = (weight_row * hidden.astype(jnp.float32)).astype(jnp.bfloat16)
    coarse = pool_sum(message, parent).astype(jnp.bfloat16)
    pre_mid = mixdot(weight_mid, coarse) + biases[1][:, None]
    coarse_out = jax.nn.silu(pre_mid).astype(jnp.bfloat16)
    merged = (hidden.astype(jnp.float32) + weight_row * coarse_out[:, parent].astype(jnp.float32)).astype(jnp.bfloat16)
    out_sum, terms_out = cheb_forward(merged, weight_out, tiles, columns)
    result = out_sum.astype(jnp.bfloat16)
    merged_grad = cheb_backward(out_grad, weight_out, tiles, columns).astype(jnp.bfloat16)
    coarse_grad = pool_sum((weight_row * merged_grad.astype(jnp.float32)).astype(jnp.bfloat16), parent)
    mid_grad = (coarse_grad * silu_slope(pre_mid)).astype(jnp.bfloat16)
    coarse_back = mixdot(weight_mid.T, mid_grad).astype(jnp.bfloat16)
    hidden_grad = merged_grad.astype(jnp.float32) + weight_row * coarse_back[:, parent].astype(jnp.float32)
    pre_grad = (hidden_grad * silu_slope(pre_in)).astype(jnp.bfloat16)
    input_grad = cheb_backward(pre_grad, weight_in, tiles, columns).astype(jnp.bfloat16)
    grads = [outer_sum(pre_grad, term) for term in terms_in]
    grads.append(outer_sum(mid_grad, coarse))
    grads = grads + [outer_sum(out_grad, term) for term in terms_out]
    bias_terms = jnp.stack([lax.optimization_barrier(jnp.sum(pre_grad.astype(jnp.float32), axis=1)), lax.optimization_barrier(jnp.sum(mid_grad.astype(jnp.float32), axis=1))])
    return (result, input_grad, jnp.stack(grads), bias_terms)

def reference(features, lap_tiles, tile_cols, coarse_owner, coarse_slot, pool_weight, weight_in, weight_mid, weight_out, biases, out_grad):
    count = features.shape[0]
    shared = lambda value: jnp.broadcast_to(value, (count,) + value.shape)
    result, input_grad, grads, bias_terms = lax.map(replica, (features, lap_tiles, tile_cols, coarse_owner, coarse_slot, pool_weight, shared(weight_in), shared(weight_mid), shared(weight_out), shared(biases), out_grad))
    factor = 1.0 / jnp.sqrt(jnp.float32(GEOS * NF))
    return (result, input_grad, lax.optimization_barrier(jnp.sum(grads, axis=0)) * factor, lax.optimization_barrier(jnp.sum(bias_terms, axis=0)) * factor)
```

```python
import math

import jax
import jax.numpy as jnp
from jax import lax
from jax.sharding import PartitionSpec as P

LINE = ("region", "sub")
BF = jnp.bfloat16
F32 = jnp.float32


def shifted(value, by):
    peers = lax.axis_size(LINE)
    pairs = [(i, i + by) for i in range(peers) if 0 <= i + by < peers]
    return lax.ppermute(value, LINE, pairs)


def placed_hot(columns, count):
    return columns.reshape(-1)[:, None] == jnp.arange(count + 2, dtype=jnp.int32)[None, :]


def forward_product(blocks, hot, tiles):
    chans = blocks.shape[0]
    count, nonzero, width = tiles.shape[:3]
    picked = jnp.einsum("cmt,jm->cjt", blocks, hot, preferred_element_type=F32).astype(BF)
    picked = picked.reshape(chans, count, nonzero, width)
    return jnp.einsum("cknt,kntu->cku", picked, tiles, preferred_element_type=F32)


def transpose_product(blocks, hot, tiles):
    chans = blocks.shape[0]
    count, nonzero, width = tiles.shape[:3]
    contrib = jnp.einsum("cku,kntu->cknt", blocks, tiles, preferred_element_type=F32)
    contrib = contrib.reshape(chans, count * nonzero, width)
    return jnp.einsum("cjt,jm->cmt", contrib, hot.astype(F32), precision=lax.Precision.HIGHEST)


def halo_round(field, extended):
    chans = field.shape[0]
    ext = extended.astype(BF)
    up = shifted(jnp.concatenate([field[:, -1], ext[:, -1]], axis=0), 1)
    down = shifted(jnp.concatenate([field[:, 0], ext[:, 0]], axis=0), -1)
    blocks = jnp.concatenate([up[:chans, None], field, down[:chans, None]], axis=1)
    inner = extended[:, 1:-1]
    inner = inner.at[:, 0].add(up[chans:].astype(F32)).at[:, -1].add(down[chans:].astype(F32))
    return blocks, inner


def both_terms(field, grad, tiles, columns):
    chans, rows = field.shape
    count, nonzero, width = tiles.shape[:3]
    hot = placed_hot(columns, count)
    hot_b = hot.astype(BF)
    f0 = field.reshape(chans, count, width)
    g0 = grad.reshape(chans, count, width)
    blocks, inner = halo_round(f0, transpose_product(g0, hot, tiles))
    f1 = forward_product(blocks, hot_b, tiles).astype(BF)
    g1 = inner.astype(BF)
    blocks, inner = halo_round(f1, transpose_product(g1, hot, tiles))
    f2 = (2.0 * forward_product(blocks, hot_b, tiles) - f0.astype(F32)).astype(BF)
    g2 = (2.0 * inner - g0.astype(F32)).astype(BF)
    stack = lambda *a: jnp.concatenate(a, axis=0).reshape(3 * chans, rows)
    return stack(f0, f1, f2), stack(g0, g1, g2)


def mixdot(weight, field):
    return jnp.dot(weight, field, preferred_element_type=F32)


def silu_slope(value):
    sig = jax.nn.sigmoid(value)
    return sig * (1.0 + value * (1.0 - sig))


def outer_sum(left, right):
    return jnp.einsum("cn,dn->cd", left, right, preferred_element_type=F32)


def spread(values, axes):
    peers = lax.axis_size(axes)
    return lax.all_to_all(
        jnp.broadcast_to(values[None], (peers, *values.shape)), axes, 0, 0, tiled=True
    )


def summed_everywhere(flat):
    regions = lax.axis_size("region")
    size = flat.shape[0]
    lanes = 128
    chunk = -(-size // (regions * lanes))
    padded = jnp.pad(flat, (0, regions * chunk * lanes - size)).reshape(regions, chunk, lanes)
    mine = jnp.sum(lax.all_to_all(padded, "region", 0, 0, tiled=True), axis=0)
    mine = jnp.sum(spread(mine, ("geo", "sub")), axis=0)
    return spread(mine, "region").reshape(-1)[:size]


def pack_slots(message, own_hot, rank_hot):
    chans = message.shape[0]
    masked = message[:, None, :] * own_hot[None, :, :]
    packed = jnp.einsum("coi,ir->cor", masked, rank_hot, preferred_element_type=F32)
    return packed.astype(BF)


def exchanged(buffer):
    return lax.all_to_all(buffer, LINE, split_axis=1, concat_axis=1, tiled=True)


def on_device(
    features,
    lap_tiles,
    tile_cols,
    coarse_owner,
    coarse_slot,
    pool_weight,
    weight_in,
    weight_mid,
    weight_out,
    biases,
    out_grad,
):
    field = features[0]
    tiles = lap_tiles[0]
    columns = tile_cols[0]
    owners = coarse_owner[0, :, 0]
    parents = coarse_slot[0]
    weight_row = pool_weight[0][None, :]
    upstream = out_grad[0]
    chans, rows = field.shape
    peers = lax.axis_size(LINE)
    slots = 4 * rows // peers
    coarse_rows = rows // 4
    own_hot = (owners[None, :] == jnp.arange(peers, dtype=jnp.int32)[:, None]).astype(BF)
    positions = jnp.arange(rows, dtype=jnp.int32)
    same_owner = (owners[:, None] == owners[None, :]) & (positions[None, :] < positions[:, None])
    rank = jnp.sum(same_owner.astype(jnp.int32), axis=1)
    rank_hot = (rank[:, None] == jnp.arange(slots, dtype=jnp.int32)[None, :]).astype(BF)
    base = 32
    ids = parents + 1
    id_rows = jnp.stack([ids // base, ids % base], axis=0).astype(BF)
    mix_in = jnp.concatenate([weight_in[k] for k in range(3)], axis=1)
    mix_out = jnp.concatenate([weight_out[k] for k in range(3)], axis=1)
    mix_in_t = jnp.concatenate([weight_in[k].T for k in range(3)], axis=1)
    mix_out_t = jnp.concatenate([weight_out[k].T for k in range(3)], axis=1)
    terms_in, terms_grad = both_terms(field, upstream, tiles, columns)
    pre_in = mixdot(mix_in, terms_in) + biases[0][:, None]
    hidden = jax.nn.silu(pre_in).astype(BF)
    message = (weight_row * hidden.astype(F32)).astype(BF)
    merged_grad = mixdot(mix_out_t, terms_grad).astype(BF)
    grad_message = (weight_row * merged_grad.astype(F32)).astype(BF)
    sent = jnp.concatenate([message, grad_message, id_rows], axis=0)
    got = exchanged(pack_slots(sent, own_hot, rank_hot))
    flat = got.reshape(2 * chans + 2, peers * slots)
    got_ids = (
        flat[2 * chans].astype(jnp.int32) * base + flat[2 * chans + 1].astype(jnp.int32) - 1
    )
    coarse_hot = (
        got_ids[:, None] == jnp.arange(coarse_rows, dtype=jnp.int32)[None, :]
    ).astype(BF)
    totals = mixdot(flat[: 2 * chans], coarse_hot)
    coarse = totals[:chans].astype(BF)
    coarse_grad = totals[chans:]
    pre_mid = mixdot(weight_mid, coarse) + biases[1][:, None]
    coarse_out = jax.nn.silu(pre_mid).astype(BF)
    mid_grad = (coarse_grad * silu_slope(pre_mid)).astype(BF)
    coarse_back = mixdot(weight_mid.T, mid_grad).astype(BF)
    values = jnp.concatenate([coarse_out, coarse_back], axis=0)
    buffer = jnp.einsum("cj,sj->cs", values, coarse_hot, preferred_element_type=F32).astype(BF)
    back = exchanged(buffer.reshape(2 * chans, peers, slots))
    lifted_all = jnp.einsum("cor,ir->coi", back, rank_hot, preferred_element_type=F32)
    lifted_all = jnp.sum(lifted_all * own_hot.astype(F32)[None, :, :], axis=1)
    lifted = lifted_all[:chans]
    lifted_grad = lifted_all[chans:]
    merged = (hidden.astype(F32) + weight_row * lifted).astype(BF)
    hidden_grad = merged_grad.astype(F32) + weight_row * lifted_grad
    pre_grad = (hidden_grad * silu_slope(pre_in)).astype(BF)
    grads_in = outer_sum(terms_in, pre_grad).reshape(3, chans, chans).transpose(0, 2, 1)
    grads_mid = outer_sum(mid_grad, coarse)
    grads_out = outer_sum(terms_grad, merged).reshape(3, chans, chans)
    local = jnp.concatenate(
        [
            grads_in.ravel(),
            grads_mid.ravel(),
            grads_out.ravel(),
            jnp.sum(pre_grad.astype(F32), axis=1),
            jnp.sum(mid_grad.astype(F32), axis=1),
        ]
    )
    factor = 1.0 / math.sqrt(lax.axis_size("geo") * rows * peers)
    total = summed_everywhere(local) * factor
    sum_weights = total[: 7 * chans * chans].reshape(7, chans, chans)
    sum_biases = total[7 * chans * chans :].reshape(2, chans)
    terms_out, terms_back = both_terms(merged, pre_grad, tiles, columns)
    result = mixdot(mix_out, terms_out).astype(BF)
    input_grad = mixdot(mix_in_t, terms_back).astype(BF)
    return (result[None], input_grad[None], sum_weights, sum_biases)


def solution(mesh):
    line = ("region", "sub")
    in_specs = (
        P("geo", None, line),
        P("geo", line, None, None, None),
        P("geo", line, None),
        P("geo", line, None),
        P("geo", line),
        P("geo", line),
        P(),
        P(),
        P(),
        P(),
        P("geo", None, line),
    )
    out_specs = (P("geo", None, line), P("geo", None, line), P(), P())
    return jax.shard_map(
        on_device, mesh=mesh, in_specs=in_specs, out_specs=out_specs, check_vma=False
    )
```

```python
import functools
import math

import jax
import jax.numpy as jnp
from jax import lax
from jax.experimental import pallas as pl
from jax.experimental.pallas import tpu as pltpu
from jax.sharding import PartitionSpec as P

LINE = ("region", "sub")
BF = jnp.bfloat16
F32 = jnp.float32
I32 = jnp.int32
LANES = 128
AUX = 8

VM = pl.BlockSpec(memory_space=pltpu.VMEM)
SM = pl.BlockSpec(memory_space=pltpu.SMEM)


def call(body, outs, scratch, args, smem=0, flops=0, limit=24):
    specs = [SM] * smem + [VM] * (len(args) - smem)
    moved = sum(a.size * a.dtype.itemsize for a in args)
    return pl.pallas_call(
        body,
        out_shape=tuple(jax.ShapeDtypeStruct(s, d) for s, d in outs),
        in_specs=specs,
        out_specs=tuple(VM for _ in outs),
        scratch_shapes=scratch,
        cost_estimate=pl.CostEstimate(flops=flops, bytes_accessed=moved, transcendentals=0),
        compiler_params=pltpu.CompilerParams(vmem_limit_bytes=limit << 20),
    )(*args)


def dot(a, b):
    return jnp.dot(a, b, preferred_element_type=F32)


def dot_nt(a, b):
    return lax.dot_general(a, b, (((1,), (1,)), ((), ())), preferred_element_type=F32)


def tile(ref, k):
    return ref[:, k * LANES : (k + 1) * LANES]


def shifted(value, by):
    peers = lax.axis_size(LINE)
    pairs = [(i, i + by) for i in range(peers) if 0 <= i + by < peers]
    return lax.ppermute(value, LINE, pairs)


def add_transposed(cols, tiles, grad_of, ext, count, nonzero):
    ext[...] = jnp.zeros_like(ext)
    for k in range(count):
        rhs = tiles[k * nonzero : (k + 1) * nonzero].reshape(nonzero * LANES, LANES)
        y = dot_nt(grad_of(k), rhs)
        for n in range(nonzero):
            ext[cols[k * nonzero + n]] += y[:, n * LANES : (n + 1) * LANES]


def row_product(cols, tiles, blocks, k, nonzero):
    picked = [blocks[cols[k * nonzero + n]] for n in range(nonzero)]
    rhs = tiles[k * nonzero : (k + 1) * nonzero].reshape(nonzero * LANES, LANES)
    return dot(jnp.concatenate(picked, axis=1), rhs)


def fill_blocks(blocks, field, up, down, chans, count):
    blocks[0] = up[0:chans, :]
    blocks[count + 1] = down[0:chans, :]
    for k in range(count):
        blocks[k + 1] = tile(field, k)


def write_sends(up, down, first, last, ext, chans, count):
    up[0:chans, :] = last
    up[chans : 2 * chans, :] = ext[count + 1].astype(BF)
    down[0:chans, :] = first
    down[chans : 2 * chans, :] = ext[0].astype(BF)


def inner_tile(inner, up, down, k, chans, count):
    value = tile(inner, k)
    if k == 0:
        value = value + up[chans : 2 * chans, :].astype(F32)
    if k == count - 1:
        value = value + down[chans : 2 * chans, :].astype(F32)
    return value


def start_body(cols, tiles, f, g, up, down, inner, ext, *, chans, count, nonzero):
    add_transposed(cols, tiles, lambda k: tile(g, k), ext, count, nonzero)
    write_sends(up, down, tile(f, 0), tile(f, count - 1), ext, chans, count)
    for k in range(count):
        inner[:, k * LANES : (k + 1) * LANES] = ext[k + 1]


def middle_body(
    cols, tiles, f, up, down, inner, f1, g1, up2, down2, inner2, blocks, ext,
    *, chans, count, nonzero
):
    fill_blocks(blocks, f, up, down, chans, count)
    for k in range(count):
        g1[:, k * LANES : (k + 1) * LANES] = inner_tile(inner, up, down, k, chans, count).astype(BF)
    for k in range(count):
        f1[:, k * LANES : (k + 1) * LANES] = row_product(cols, tiles, blocks, k, nonzero).astype(BF)
    add_transposed(cols, tiles, lambda k: tile(g1, k), ext, count, nonzero)
    write_sends(up2, down2, tile(f1, 0), tile(f1, count - 1), ext, chans, count)
    for k in range(count):
        inner2[:, k * LANES : (k + 1) * LANES] = ext[k + 1]


def second_terms(cols, tiles, f, g, f1, up, down, inner, blocks, f2, g2, chans, count, nonzero):
    fill_blocks(blocks, f1, up, down, chans, count)
    for k in range(count):
        at = slice(k * LANES, (k + 1) * LANES)
        y = row_product(cols, tiles, blocks, k, nonzero)
        f2[:, at] = (2.0 * y - f[:, at].astype(F32)).astype(BF)
        z = inner_tile(inner, up, down, k, chans, count)
        g2[:, at] = (2.0 * z - g[:, at].astype(F32)).astype(BF)


def place_body(owner, slot, dest, rank, most, *, peers, rows):
    d = owner[...] + slot[...]
    d = d - (d // peers) * peers
    dest[...] = d
    hot = lax.broadcasted_iota(I32, (peers, rows), 0) == d
    hot = jnp.where(hot, 1.0, 0.0).astype(F32)
    a = lax.broadcasted_iota(I32, (LANES, LANES), 0)
    b = lax.broadcasted_iota(I32, (LANES, LANES), 1)
    before = jnp.where(a < b, 1.0, 0.0).astype(BF)
    carry = jnp.zeros((peers, 1), F32)
    for k in range(rows // LANES):
        h = hot[:, k * LANES : (k + 1) * LANES]
        c = dot(h.astype(BF), before) + carry
        rank[:, k * LANES : (k + 1) * LANES] = jnp.sum(h * c, axis=0, keepdims=True).astype(I32)
        carry = carry + jnp.sum(h, axis=1, keepdims=True)
    most[...] = jnp.broadcast_to(jnp.max(carry, axis=0, keepdims=True), (AUX, LANES))


def slot_hot(dest, rank, step, cap, go, rows):
    at = rank - step * cap
    inside = (at >= 0) & (at < cap)
    col = jnp.where(inside, (dest - (dest // go) * go) * cap + at, -1)
    hot = lax.broadcasted_iota(I32, (go * cap, rows), 0) == col
    return jnp.where(hot, 1.0, 0.0).astype(BF)


def merge_halves(low, high, odd, cap):
    if cap == LANES // 2:
        left = lax.broadcasted_iota(I32, low.shape, 1) < cap
        if odd:
            return jnp.where(left, pltpu.roll(low, cap, 1), high)
        return jnp.where(left, low, pltpu.roll(high, cap, 1))
    at = slice(cap, 2 * cap) if odd else slice(0, cap)
    return jnp.concatenate([low[:, at], high[:, at]], axis=1)


def pack_into(buffer, big, sent, dest, rank, most, step, *, chans, peers, cap, go, rows):
    high = 2 * chans + AUX
    group = dest // go
    for g in range(peers // go):
        big[g * high : (g + 1) * high, :] = jnp.where(group == g, sent, 0.0).astype(BF)
    out = dot_nt(big[...], slot_hot(dest, rank, step, cap, go, rows))
    row = lax.broadcasted_iota(I32, (AUX, 2 * cap), 0)
    lane = lax.broadcasted_iota(I32, (AUX, 2 * cap), 1)
    extra = jnp.where((row == 1) & (lane >= cap), float(LANES), 0.0)
    extra = extra + jnp.where(row == 2, most, 0.0)
    for p in range(peers):
        g, o = p // go, p % go
        pair = o // 2 * 2 * cap
        part = out[g * high : (g + 1) * high, pair : pair + 2 * cap]
        if go == 1:
            part = jnp.concatenate([out[g * high : (g + 1) * high]] * 2, axis=1)
        odd = o % 2 == 1
        buffer[p, 0:chans, :] = merge_halves(
            part[0:chans], part[chans : 2 * chans], odd, cap
        ).astype(BF)
        aux = part[2 * chans : high]
        buffer[p, chans : chans + AUX, :] = (merge_halves(aux, aux, odd, cap) + extra).astype(BF)


def pack_body(step, sent, dest, rank, most, buffer, big, *, cap, **sizes):
    needed = jnp.ceil(most[0:1, 0:1] * (1.0 / cap))
    pack_into(
        buffer, big, sent[...].astype(F32), dest[...], rank[...], needed, step[0], cap=cap, **sizes
    )


def unpack_body(step, back, dest, rank, lifted, big, *, chans, peers, cap, go, rows):
    d = dest[...]
    hot = slot_hot(d, rank[...], step[0], cap, go, rows)
    group = d // go
    high = 2 * chans
    for p in range(0, peers, 2 if go > 1 else 1):
        g, o = p // go, p % go
        a = back[p].astype(F32)
        if go == 1:
            low, top = a[:, 0:cap], a[:, cap : 2 * cap]
            at = slice(0, cap)
        else:
            b = back[p + 1].astype(F32)
            at = slice(o * cap, (o + 2) * cap)
            if cap == LANES // 2:
                low, top = merge_halves(a, b, False, cap), merge_halves(a, b, True, cap)
            else:
                low = jnp.concatenate([a[:, 0:cap], b[:, 0:cap]], axis=1)
                top = jnp.concatenate([a[:, cap:], b[:, cap:]], axis=1)
        big[g * high : g * high + chans, at] = low.astype(BF)
        big[g * high + chans : (g + 1) * high, at] = top.astype(BF)
    width = min(256, rows)
    for w in range(rows // width):
        at = slice(w * width, (w + 1) * width)
        y = dot(big[...], hot[:, at])
        total = jnp.zeros((high, width), F32)
        for g in range(peers // go):
            total = jnp.where(group[:, at] == g, y[g * high : (g + 1) * high], total)
        lifted[:, at] = total.astype(BF)


def coarse_hot(got, hot, masked, *, chans, peers, cap, parts):
    wide = 2 * cap

    def one(p, carry):
        aux = got[p, chans : chans + AUX, :].astype(F32)
        at = pl.ds(pl.multiple_of(p * wide, wide), wide)
        code = aux[1:2, :].astype(I32)
        q = lax.broadcasted_iota(I32, (2 * LANES, wide), 0)
        hot[:, at] = jnp.where(q == code, 1.0, 0.0).astype(BF)
        if masked is not None:
            body = got[p, 0:chans, :].astype(F32)
            for h in range(parts):
                masked[h * chans : (h + 1) * chans, at] = jnp.where(
                    aux[0:1, :] == h + 1.0, body, 0.0
                ).astype(BF)
        return carry

    lax.fori_loop(0, peers, one, 0, unroll=4)


def coarse_totals(hot, masked, chans, parts):
    acc = dot_nt(masked[...], hot[...])
    split = [acc[h * chans : (h + 1) * chans] for h in range(parts)]
    low = jnp.concatenate([s[:, 0:LANES] for s in split], axis=1)
    top = jnp.concatenate([s[:, LANES:] for s in split], axis=1)
    return low, top


def slope(value):
    sig = jax.nn.sigmoid(value)
    return sig * (1.0 + value * (1.0 - sig))


def coarse_math(coarse_sum, coarse_grad, weight, weight_t, bias, grads):
    coarse = coarse_sum.astype(BF)
    pre = dot(weight[...], coarse) + bias[...]
    out = (pre * jax.nn.sigmoid(pre)).astype(BF)
    mid_grad = (coarse_grad * slope(pre)).astype(BF)
    chans = pre.shape[0]
    grads[0:chans, :] = dot_nt(mid_grad, coarse)
    grads[chans : 2 * chans, :] = jnp.broadcast_to(
        jnp.sum(mid_grad.astype(F32), axis=1, keepdims=True), (chans, chans)
    )
    return out, dot(weight_t[...], mid_grad).astype(BF)


def coarse_gather(back, got, hot, out, behind, *, chans, peers, cap, parts):
    wide = 2 * cap
    stacked = [
        jnp.concatenate(
            [out[:, h * LANES : (h + 1) * LANES], behind[:, h * LANES : (h + 1) * LANES]], axis=1
        )
        for h in range(parts)
    ]
    stacked = jnp.concatenate(stacked, axis=0)
    step = max(1, 512 // wide)

    def one(b, carry):
        at = pl.ds(pl.multiple_of(b * step * wide, step * wide), step * wide)
        y = dot(stacked, hot[:, at])
        for j in range(step):
            p = b * step + j
            part = got[p, chans : chans + AUX, :].astype(F32)[0:1, :]
            total = jnp.zeros((chans, wide), F32)
            for h in range(parts):
                total = jnp.where(
                    part == h + 1.0,
                    y[h * chans : (h + 1) * chans, j * wide : (j + 1) * wide],
                    total,
                )
            back[p] = total.astype(BF)
        return carry

    lax.fori_loop(0, peers // step, one, 0, unroll=2)


def coarse_body(got, weight, weight_t, bias, back, grads, hot, masked, **sizes):
    coarse_hot(got, hot, masked, **sizes)
    low, top = coarse_totals(hot, masked, sizes["chans"], sizes["parts"])
    out, behind = coarse_math(low, top, weight, weight_t, bias, grads)
    coarse_gather(back, got, hot, out, behind, **sizes)


def totals_body(got, before, after, hot, masked, **sizes):
    chans = sizes["chans"]
    coarse_hot(got, hot, masked, **sizes)
    low, top = coarse_totals(hot, masked, chans, sizes["parts"])
    after[0:chans, :] = before[0:chans, :] + low
    after[chans : 2 * chans, :] = before[chans : 2 * chans, :] + top


def math_body(totals, weight, weight_t, bias, values, grads):
    chans = totals.shape[0] // 2
    out, behind = coarse_math(
        totals[0:chans, :], totals[chans : 2 * chans, :], weight, weight_t, bias, grads
    )
    values[0:chans, :] = out
    values[chans : 2 * chans, :] = behind


def gather_body(got, values, back, hot, **sizes):
    chans = sizes["chans"]
    coarse_hot(got, hot, None, **sizes)
    coarse_gather(
        back, got, hot, values[0:chans, :], values[chans : 2 * chans, :], **sizes
    )


def first_end_body(
    cols, tiles, f, g, f1, g1, up, down, inner, pool, mix_in, mix_out_t, bias,
    dest, rank, most, slot, owner,
    f2, g2, pre_in, hidden, merged_grad, sent, buffer, blocks, big,
    *, chans, count, nonzero, peers, cap, go, rows
):
    second_terms(cols, tiles, f, g, f1, up, down, inner, blocks, f2, g2, chans, count, nonzero)
    for k in range(count):
        at = slice(k * LANES, (k + 1) * LANES)
        w = pool[:, at]
        pre = dot(mix_in[...], jnp.concatenate([f[:, at], f1[:, at], f2[:, at]], axis=0)) + bias[...]
        pre_in[:, at] = pre
        h = (pre * jax.nn.sigmoid(pre)).astype(BF)
        hidden[:, at] = h
        m = dot(mix_out_t[...], jnp.concatenate([g[:, at], g1[:, at], g2[:, at]], axis=0)).astype(BF)
        merged_grad[:, at] = m
        sent[0:chans, at] = (w * h.astype(F32)).astype(BF)
        sent[chans : 2 * chans, at] = (w * m.astype(F32)).astype(BF)
    each = rows // 4 // peers
    index = owner[...] * each + slot[...] // peers
    part = index // LANES
    row = lax.broadcasted_iota(I32, (AUX, rows), 0)
    sent[2 * chans : 2 * chans + AUX, :] = (
        jnp.where(row == 0, part + 1, jnp.where(row == 1, index - part * LANES, 0))
        .astype(F32)
        .astype(BF)
    )
    needed = jnp.ceil(most[0:1, 0:1] * (1.0 / cap))
    pack_into(
        buffer, big, sent[...].astype(F32), dest[...], rank[...], needed, 0,
        chans=chans, peers=peers, cap=cap, go=go, rows=rows,
    )


def second_start_body(
    cols, tiles, lifted, hidden, merged_grad, pre_in, pool,
    merged, pre_grad, up, down, inner, ext,
    *, chans, count, nonzero
):
    for k in range(count):
        at = slice(k * LANES, (k + 1) * LANES)
        w = pool[:, at]
        merged[:, at] = (
            hidden[:, at].astype(F32) + w * lifted[0:chans, at].astype(F32)
        ).astype(BF)
        hidden_grad = merged_grad[:, at].astype(F32) + w * lifted[chans : 2 * chans, at].astype(F32)
        pre_grad[:, at] = (hidden_grad * slope(pre_in[:, at])).astype(BF)
    add_transposed(cols, tiles, lambda k: tile(pre_grad, k), ext, count, nonzero)
    write_sends(up, down, tile(merged, 0), tile(merged, count - 1), ext, chans, count)
    for k in range(count):
        inner[:, k * LANES : (k + 1) * LANES] = ext[k + 1]


def weights_body(merged, pre_grad, f, f1, f2, g, g1, g2, mid, local, *, chans):
    p, m = pre_grad[...], merged[...]
    gin = [dot_nt(p, t[...]) for t in (f, f1, f2)]
    gout = [dot_nt(t[...], m) for t in (g, g1, g2)]
    local[0:chans, :] = jnp.concatenate(gin + [mid[0:chans, :]], axis=1)
    total = jnp.broadcast_to(jnp.sum(p.astype(F32), axis=1, keepdims=True), (chans, chans))
    lane = lax.broadcasted_iota(I32, (chans, chans), 1)
    sums = jnp.where(lane == 0, total, mid[chans : 2 * chans, :])
    local[chans : 2 * chans, :] = jnp.concatenate(gout + [sums], axis=1)


def second_end_body(
    cols, tiles, f, g, f1, g1, up, down, inner, mix_out, mix_in_t,
    result, input_grad, f2, g2, blocks,
    *, chans, count, nonzero
):
    second_terms(cols, tiles, f, g, f1, up, down, inner, blocks, f2, g2, chans, count, nonzero)
    for k in range(count):
        at = slice(k * LANES, (k + 1) * LANES)
        terms = jnp.concatenate([f[:, at], f1[:, at], f2[:, at]], axis=0)
        result[:, at] = dot(mix_out[...], terms).astype(BF)
        terms = jnp.concatenate([g[:, at], g1[:, at], g2[:, at]], axis=0)
        input_grad[:, at] = dot(mix_in_t[...], terms).astype(BF)


def spread(values, axes):
    peers = lax.axis_size(axes)
    return lax.all_to_all(
        jnp.broadcast_to(values[None], (peers, *values.shape)), axes, 0, 0, tiled=True
    )


def summed_everywhere(local):
    regions = lax.axis_size("region")
    parts = local.reshape(regions, -1, LANES)
    mine = jnp.sum(lax.all_to_all(parts, "region", 0, 0, tiled=True), axis=0)
    mine = jnp.sum(spread(mine, ("geo", "sub")), axis=0)
    return spread(mine, "region").reshape(local.shape)


def exchanged(buffer):
    return lax.all_to_all(buffer, LINE, 0, 0, tiled=True)


def on_device(
    features,
    lap_tiles,
    tile_cols,
    coarse_owner,
    coarse_slot,
    pool_weight,
    weight_in,
    weight_mid,
    weight_out,
    biases,
    out_grad,
):
    chans, rows = features.shape[1:]
    count, nonzero = lap_tiles.shape[1:3]
    peers = lax.axis_size(LINE)
    cap = 2 * rows // peers
    go = max(1, 256 // cap)
    coarse_rows = rows // 4
    parts = coarse_rows // LANES
    f, g = features[0], out_grad[0]
    tiles = lap_tiles[0].reshape(count * nonzero, LANES, LANES)
    cols = tile_cols[0].reshape(-1)
    owner = coarse_owner[0].reshape(1, rows)
    slot = coarse_slot
    pool = pool_weight
    side = lambda w: jnp.concatenate([w[k] for k in range(3)], axis=1)
    side_t = lambda w: jnp.concatenate([w[k].T for k in range(3)], axis=1)
    line = dict(chans=chans, count=count, nonzero=nonzero)
    ways = dict(chans=chans, peers=peers, cap=cap, go=go, rows=rows)
    level = dict(chans=chans, peers=peers, cap=cap, parts=parts)
    full = (chans, rows)
    halo = (2 * chans, LANES)
    ext = pltpu.VMEM((count + 2, chans, LANES), F32)
    blocks = pltpu.VMEM((count + 2, chans, LANES), BF)
    work = 2 * chans * rows * nonzero * LANES
    chunk = (peers, chans + AUX, 2 * cap)
    reply = (peers, chans, 2 * cap)
    hot_s = pltpu.VMEM((2 * LANES, peers * 2 * cap), BF)
    masked_s = pltpu.VMEM((parts * chans, peers * 2 * cap), BF)
    pack_s = pltpu.VMEM((peers // go * (2 * chans + AUX), rows), BF)
    lift_s = pltpu.VMEM((peers // go * 2 * chans, go * cap), BF)

    up, down, inner = call(
        functools.partial(start_body, **line),
        [(halo, BF), (halo, BF), (full, F32)],
        [ext],
        (cols, tiles, f, g),
        smem=1,
        flops=work,
    )
    up, down = shifted(up, 1), shifted(down, -1)
    dest, rank, most = call(
        functools.partial(place_body, peers=peers, rows=rows),
        [((1, rows), I32), ((1, rows), I32), ((AUX, LANES), F32)],
        [],
        (owner, slot),
        flops=2 * work,
    )
    f1, g1, up, down, inner = call(
        functools.partial(middle_body, **line),
        [(full, BF), (full, BF), (halo, BF), (halo, BF), (full, F32)],
        [blocks, ext],
        (cols, tiles, f, up, down, inner),
        smem=1,
        flops=2 * work,
    )
    up, down = shifted(up, 1), shifted(down, -1)
    f2, g2, pre_in, hidden, merged_grad, sent, buffer = call(
        functools.partial(first_end_body, **line, peers=peers, cap=cap, go=go, rows=rows),
        [
            (full, BF),
            (full, BF),
            (full, F32),
            (full, BF),
            (full, BF),
            ((2 * chans + AUX, rows), BF),
            (chunk, BF),
        ],
        [blocks, pack_s],
        (
            cols, tiles, f, g, f1, g1, up, down, inner, pool, side(weight_in), side_t(weight_out),
            biases[0][:, None], dest, rank, most, slot, owner,
        ),
        smem=1,
        flops=4 * work,
        limit=32,
    )
    got = exchanged(buffer)
    rounds = jnp.max(got[:, chans + 2, 0].astype(F32)).astype(I32)
    bias_mid = biases[1][:, None]
    weight_mid_t = weight_mid.T

    def unpacked(back, step):
        return call(
            functools.partial(unpack_body, **ways),
            [((2 * chans, rows), BF)],
            [lift_s],
            (step, back, dest, rank),
            smem=1,
        )[0]

    def one_round(got):
        back, grads = call(
            functools.partial(coarse_body, **level),
            [(reply, BF), ((2 * chans, chans), F32)],
            [hot_s, masked_s],
            (got, weight_mid, weight_mid_t, bias_mid),
            limit=32,
        )
        return unpacked(exchanged(back), jnp.zeros((1,), I32)), grads

    def more_rounds(got):
        def received(step):
            return exchanged(
                call(
                    functools.partial(pack_body, **ways),
                    [(chunk, BF)],
                    [pack_s],
                    (step.reshape(1), sent, dest, rank, most),
                    smem=1,
                    limit=32,
                )[0]
            )

        def add(step, totals):
            return call(
                functools.partial(totals_body, **level),
                [((2 * chans, coarse_rows), F32)],
                [hot_s, masked_s],
                (received(step), totals),
                limit=32,
            )[0]

        totals = lax.fori_loop(0, rounds, add, jnp.zeros((2 * chans, coarse_rows), F32))
        values, grads = call(
            math_body,
            [((2 * chans, coarse_rows), BF), ((2 * chans, chans), F32)],
            [],
            (totals, weight_mid, weight_mid_t, bias_mid),
        )

        def fetch(step, lifted):
            back = call(
                functools.partial(gather_body, **level),
                [(reply, BF)],
                [hot_s],
                (received(step), values),
                limit=32,
            )[0]
            return lifted + unpacked(exchanged(back), step.reshape(1))

        return lax.fori_loop(0, rounds, fetch, jnp.zeros((2 * chans, rows), BF)), grads

    lifted, mid = lax.cond(rounds > 1, more_rounds, one_round, got)

    merged, pre_grad, up, down, inner = call(
        functools.partial(second_start_body, **line),
        [(full, BF), (full, BF), (halo, BF), (halo, BF), (full, F32)],
        [ext],
        (cols, tiles, lifted, hidden, merged_grad, pre_in, pool),
        smem=1,
        flops=work,
    )
    up, down = shifted(up, 1), shifted(down, -1)
    local = call(
        functools.partial(weights_body, chans=chans),
        [((2 * chans, LANES), F32)],
        [],
        (merged, pre_grad, f, f1, f2, g, g1, g2, mid),
        flops=work,
    )[0]
    m1, p1, up, down, inner = call(
        functools.partial(middle_body, **line),
        [(full, BF), (full, BF), (halo, BF), (halo, BF), (full, F32)],
        [blocks, ext],
        (cols, tiles, merged, up, down, inner),
        smem=1,
        flops=2 * work,
    )
    up, down = shifted(up, 1), shifted(down, -1)
    result, input_grad = call(
        functools.partial(second_end_body, **line),
        [(full, BF), (full, BF)],
        [pltpu.VMEM(full, BF), pltpu.VMEM(full, BF), blocks],
        (
            cols, tiles, merged, pre_grad, m1, p1, up, down, inner,
            side(weight_out), side_t(weight_in),
        ),
        smem=1,
        flops=2 * work,
    )
    factor = 1.0 / math.sqrt(lax.axis_size("geo") * rows * peers)
    total = summed_everywhere(local) * factor
    first = total[:chans].reshape(chans, 4, chans).transpose(1, 0, 2)
    second = total[chans:].reshape(chans, 4, chans).transpose(1, 0, 2)
    sum_weights = jnp.concatenate([first, second[:3]], axis=0)
    sum_biases = second[3, :, :2].T
    return (result[None], input_grad[None], sum_weights, sum_biases)


def solution(mesh):
    line = ("region", "sub")
    in_specs = (
        P("geo", None, line),
        P("geo", line, None, None, None),
        P("geo", line, None),
        P("geo", line, None),
        P("geo", line),
        P("geo", line),
        P(),
        P(),
        P(),
        P(),
        P("geo", None, line),
    )
    out_specs = (P("geo", None, line), P("geo", None, line), P(), P())
    return jax.shard_map(
        on_device, mesh=mesh, in_specs=in_specs, out_specs=out_specs, check_vma=False
    )
```

```python
import functools
import math

import jax
import jax.numpy as jnp
from jax import lax
from jax.experimental import pallas as pl
from jax.experimental.pallas import tpu as pltpu
from jax.sharding import PartitionSpec as P


LINE = ("region", "sub")
BF = jnp.bfloat16
F32 = jnp.float32
I32 = jnp.int32
LANES = 128
AUX = 8
PAD = 16
START_LIMIT = 59

VM = pl.BlockSpec(memory_space=pltpu.VMEM)
SM = pl.BlockSpec(memory_space=pltpu.SMEM)
HB = pl.BlockSpec(memory_space=pltpu.HBM)


def call(body, outs, scratch, args, smem=0, flops=0, limit=24, far=(), far_out=()):
    specs = [SM] * smem + [VM] * (len(args) - smem)
    for i in far:
        specs[i] = HB
    moved = sum(a.size * a.dtype.itemsize for a in args)
    return pl.pallas_call(
        body,
        out_shape=tuple(jax.ShapeDtypeStruct(s, d) for s, d in outs),
        in_specs=specs,
        out_specs=tuple(HB if i in far_out else VM for i in range(len(outs))),
        scratch_shapes=scratch,
        cost_estimate=pl.CostEstimate(flops=flops, bytes_accessed=moved, transcendentals=0),
        compiler_params=pltpu.CompilerParams(vmem_limit_bytes=limit << 20),
    )(*args)


def dot(a, b):
    return jnp.dot(a, b, preferred_element_type=F32)


def dot_nt(a, b):
    return lax.dot_general(a, b, (((1,), (1,)), ((), ())), preferred_element_type=F32)


def lanes(k):
    if isinstance(k, int):
        return slice(k * LANES, (k + 1) * LANES)
    return pl.ds(pl.multiple_of(k * LANES, LANES), LANES)


def tile(ref, k):
    return ref[:, lanes(k)]


def each(count, one, compact):
    if not compact:
        for k in range(count):
            one(k)
        return

    def body(k, carry):
        one(k)
        return carry

    lax.fori_loop(0, count, body, 0)


def shifted(value, by):
    peers = lax.axis_size(LINE)
    pairs = [(i, i + by) for i in range(peers) if 0 <= i + by < peers]
    return lax.ppermute(value, LINE, pairs)


def fetched(tiles_h, tiles, sems, count, nonzero, compact):
    pieces = 4 if count % 4 == 0 else 1
    size = count // pieces
    copies = []
    for i in range(pieces):
        at = slice(i * size * nonzero, (i + 1) * size * nonzero)
        copies.append(pltpu.make_async_copy(tiles_h.at[at], tiles.at[at], sems.at[i]))
        copies[-1].start()

    if compact:
        for c in copies:
            c.wait()

    def ready(k):
        if not compact and k % size == 0:
            copies[k // size].wait()

    return ready


def add_transposed(cols, tiles, grad_of, ext, count, nonzero, compact):
    ext[...] = jnp.zeros_like(ext)

    def one(k):
        y = dot_nt(grad_of(k), row_tiles(tiles, k, nonzero))
        for n in range(nonzero):
            ext[cols[k, n]] += y[:, n * LANES : (n + 1) * LANES]

    each(count, one, compact)


def row_tiles(tiles, k, nonzero):
    return tiles[pl.ds(k * nonzero, nonzero)].reshape(nonzero * LANES, LANES)


def row_product(cols, tiles, blocks, k, nonzero):
    picked = [blocks[cols[k, n]] for n in range(nonzero)]
    return dot(jnp.concatenate(picked, axis=1), row_tiles(tiles, k, nonzero))


def fill_blocks(blocks, field, up, down, chans, count, compact):
    blocks[0] = up[0:chans, :]
    blocks[count + 1] = down[0:chans, :]

    def one(k):
        blocks[k + 1] = tile(field, k)

    each(count, one, compact)


def write_sends(up, down, first, last, ext, chans, count):
    up[0:chans, :] = last
    up[chans : 2 * chans, :] = ext[count + 1].astype(BF)
    down[0:chans, :] = first
    down[chans : 2 * chans, :] = ext[0].astype(BF)


def inner_tile(inner, up, down, k, chans, count):
    value = tile(inner, k)
    if not isinstance(k, int):
        first = jnp.where(k == 0, 1.0, 0.0)
        last = jnp.where(k == count - 1, 1.0, 0.0)
        value = value + first * up[chans : 2 * chans, :].astype(F32)
        return value + last * down[chans : 2 * chans, :].astype(F32)
    if k == 0:
        value = value + up[chans : 2 * chans, :].astype(F32)
    if k == count - 1:
        value = value + down[chans : 2 * chans, :].astype(F32)
    return value


def start_body(
    cols, tiles_h, f_h, g_h, up, down, inner, ext, tiles, edge, g, sems, *, chans, count, nonzero, compact
):
    last = slice((count - 1) * LANES, count * LANES)
    copies = [
        pltpu.make_async_copy(g_h, g, sems.at[4]),
        pltpu.make_async_copy(f_h.at[:, 0:LANES], edge.at[0], sems.at[5]),
        pltpu.make_async_copy(f_h.at[:, last], edge.at[1], sems.at[6]),
    ]
    copies[0].start()
    ready = fetched(tiles_h, tiles, sems, count, nonzero, compact)
    copies[1].start()
    copies[2].start()
    copies[0].wait()

    def grad_of(k):
        ready(k)
        return tile(g, k)

    add_transposed(cols, tiles, grad_of, ext, count, nonzero, compact)
    copies[1].wait()
    copies[2].wait()
    write_sends(up, down, edge[0], edge[1], ext, chans, count)

    def one(k):
        inner[:, lanes(k)] = ext[k + 1]

    each(count, one, compact)


def middle_body(
    cols, tiles_h, f, up, down, inner, f1, g1, up2, down2, inner2, blocks, ext, tiles, sems,
    *, chans, count, nonzero, compact
):
    ready = fetched(tiles_h, tiles, sems, count, nonzero, compact)
    fill_blocks(blocks, f, up, down, chans, count, compact)

    def one(k):
        g1[:, lanes(k)] = inner_tile(inner, up, down, k, chans, count).astype(BF)

    each(count, one, compact)

    def one(k):
        ready(k)
        f1[:, lanes(k)] = row_product(cols, tiles, blocks, k, nonzero).astype(BF)

    each(count, one, compact)
    add_transposed(cols, tiles, lambda k: tile(g1, k), ext, count, nonzero, compact)
    write_sends(up2, down2, tile(f1, 0), tile(f1, count - 1), ext, chans, count)

    def one(k):
        inner2[:, lanes(k)] = ext[k + 1]

    each(count, one, compact)


def second_terms(
    cols, tiles, f, g, f1, up, down, inner, blocks, f2, g2, chans, count, nonzero, ready, compact
):
    fill_blocks(blocks, f1, up, down, chans, count, compact)

    def one(k):
        ready(k)
        at = lanes(k)
        y = row_product(cols, tiles, blocks, k, nonzero)
        f2[:, at] = (2.0 * y - f[:, at].astype(F32)).astype(BF)
        z = inner_tile(inner, up, down, k, chans, count)
        g2[:, at] = (2.0 * z - g[:, at].astype(F32)).astype(BF)

    each(count, one, compact)


def place_body(owner, slot, dest, rank, most, *, peers, rows):
    d = owner[...] + slot[...]
    d = d - (d // peers) * peers
    dest[...] = d
    hot = lax.broadcasted_iota(I32, (peers, rows), 0) == d
    hot = jnp.where(hot, 1.0, 0.0).astype(F32)
    a = lax.broadcasted_iota(I32, (LANES, LANES), 0)
    b = lax.broadcasted_iota(I32, (LANES, LANES), 1)
    before = jnp.where(a < b, 1.0, 0.0).astype(BF)
    carry = jnp.zeros((peers, 1), F32)
    for k in range(rows // LANES):
        h = hot[:, k * LANES : (k + 1) * LANES]
        c = dot(h.astype(BF), before) + carry
        rank[:, k * LANES : (k + 1) * LANES] = jnp.sum(h * c, axis=0, keepdims=True).astype(I32)
        carry = carry + jnp.sum(h, axis=1, keepdims=True)
    most[...] = jnp.broadcast_to(jnp.max(carry, axis=0, keepdims=True), (AUX, LANES))


def slot_hot(dest, rank, step, cap, go, rows):
    at = rank - step * cap
    inside = (at >= 0) & (at < cap)
    col = jnp.where(inside, (dest - (dest // go) * go) * cap + at, -1)
    hot = lax.broadcasted_iota(I32, (go * cap, rows), 0) == col
    return jnp.where(hot, 1.0, 0.0).astype(BF)


def merge_halves(low, high, odd, cap):
    if cap == LANES // 2:
        left = lax.broadcasted_iota(I32, low.shape, 1) < cap
        if odd:
            return jnp.where(left, pltpu.roll(low, cap, 1), high)
        return jnp.where(left, low, pltpu.roll(high, cap, 1))
    at = slice(cap, 2 * cap) if odd else slice(0, cap)
    return jnp.concatenate([low[:, at], high[:, at]], axis=1)


def pack_into(
    buffer, big, out, sent, dest, rank, most, step, *, chans, peers, cap, go, rows
):
    high = 2 * chans + PAD
    group = dest // go

    def mask(g, carry):
        here = jnp.where(group == g, 1.0, 0.0).astype(BF)
        big[pl.ds(pl.multiple_of(g * high, high), high), :] = sent[...] * here
        return carry

    lax.fori_loop(0, peers // go, mask, 0, unroll=2)
    out[...] = dot_nt(big[...], slot_hot(dest, rank, step, cap, go, rows))
    row = lax.broadcasted_iota(I32, (AUX, 2 * cap), 0)
    lane = lax.broadcasted_iota(I32, (AUX, 2 * cap), 1)
    extra = jnp.where((row == 1) & (lane >= cap), float(LANES), 0.0)
    extra = extra + jnp.where(row == 2, most, 0.0)

    def place(g, carry):
        part = out[pl.ds(pl.multiple_of(g * high, high), high), :]
        for o in range(go):
            pair = o // 2 * 2 * cap
            near = jnp.concatenate([part] * 2, axis=1) if go == 1 else part[:, pair : pair + 2 * cap]
            odd = o % 2 == 1
            p = g * go + o
            body = merge_halves(near[0:chans], near[chans : 2 * chans], odd, cap)
            buffer[p, 0:chans, :] = body.astype(BF)
            aux = near[2 * chans : 2 * chans + AUX]
            buffer[p, chans : chans + AUX, :] = (merge_halves(aux, aux, odd, cap) + extra).astype(BF)
        return carry

    lax.fori_loop(0, peers // go, place, 0, unroll=2)


def pack_body(step, sent, dest, rank, most, buffer, big, out, *, cap, **sizes):
    needed = jnp.ceil(most[0:1, 0:1] * (1.0 / cap))
    pack_into(buffer, big, out, sent, dest[...], rank[...], needed, step[0], cap=cap, **sizes)


def unpack_body(step, back, dest, rank, lifted, big, hot, *, chans, peers, cap, go, rows):
    hot[...] = slot_hot(dest[...], rank[...], step[0], cap, go, rows)
    high = 2 * chans

    def gather(g, carry):
        rows_low = pl.ds(pl.multiple_of(g * high, high), chans)
        rows_top = pl.ds(pl.multiple_of(g * high + chans, chans), chans)
        for o in range(0, go, 2):
            a = back[g * go + o].astype(F32)
            if go == 1:
                low, top = a[:, 0:cap], a[:, cap : 2 * cap]
                at = slice(0, cap)
            else:
                b = back[g * go + o + 1].astype(F32)
                at = slice(o * cap, (o + 2) * cap)
                if cap == LANES // 2:
                    low, top = merge_halves(a, b, False, cap), merge_halves(a, b, True, cap)
                else:
                    low = jnp.concatenate([a[:, 0:cap], b[:, 0:cap]], axis=1)
                    top = jnp.concatenate([a[:, cap:], b[:, cap:]], axis=1)
            big[rows_low, at] = low.astype(BF)
            big[rows_top, at] = top.astype(BF)
        return carry

    lax.fori_loop(0, peers // go, gather, 0, unroll=2)
    width = min(256, rows)

    def select(w, carry):
        at = pl.ds(pl.multiple_of(w * width, width), width)
        y = dot(big[...], hot[:, at])
        group = dest[:, at] // go
        total = jnp.zeros((high, width), F32)
        for g in range(peers // go):
            total = jnp.where(group == g, y[g * high : (g + 1) * high], total)
        lifted[:, at] = total.astype(BF)
        return carry

    lax.fori_loop(0, rows // width, select, 0)


def coarse_hot(got, hot, masked, *, chans, peers, cap, parts):
    wide = 2 * cap

    def one(p, carry):
        aux = got[p, chans : chans + AUX, :].astype(F32)
        at = pl.ds(pl.multiple_of(p * wide, wide), wide)
        code = aux[1:2, :].astype(I32)
        q = lax.broadcasted_iota(I32, (2 * LANES, wide), 0)
        hot[:, at] = jnp.where(q == code, 1.0, 0.0).astype(BF)
        if masked is not None:
            body = got[p, 0:chans, :].astype(F32)
            for h in range(parts):
                masked[h * chans : (h + 1) * chans, at] = jnp.where(
                    aux[0:1, :] == h + 1.0, body, 0.0
                ).astype(BF)
        return carry

    lax.fori_loop(0, peers, one, 0, unroll=4)


def coarse_totals(hot, masked, chans, parts):
    acc = dot_nt(masked[...], hot[...])
    split = [acc[h * chans : (h + 1) * chans] for h in range(parts)]
    low = jnp.concatenate([s[:, 0:LANES] for s in split], axis=1)
    top = jnp.concatenate([s[:, LANES:] for s in split], axis=1)
    return low, top


def slope(value):
    sig = jax.nn.sigmoid(value)
    return sig * (1.0 + value * (1.0 - sig))


def coarse_math(coarse_sum, coarse_grad, weight, weight_t, bias, grads):
    coarse = coarse_sum.astype(BF)
    pre = dot(weight[...], coarse) + bias[...]
    out = (pre * jax.nn.sigmoid(pre)).astype(BF)
    mid_grad = (coarse_grad * slope(pre)).astype(BF)
    chans = pre.shape[0]
    grads[0:chans, :] = dot_nt(mid_grad, coarse)
    ones = jnp.ones((chans, mid_grad.shape[1]), BF)
    grads[chans : 2 * chans, :] = dot_nt(ones, mid_grad)
    return out, dot(weight_t[...], mid_grad).astype(BF)


def coarse_gather(back, got, hot, out, behind, *, chans, peers, cap, parts):
    wide = 2 * cap
    stacked = [
        jnp.concatenate(
            [out[:, h * LANES : (h + 1) * LANES], behind[:, h * LANES : (h + 1) * LANES]], axis=1
        )
        for h in range(parts)
    ]
    stacked = jnp.concatenate(stacked, axis=0)
    step = max(1, 512 // wide)

    def one(b, carry):
        at = pl.ds(pl.multiple_of(b * step * wide, step * wide), step * wide)
        y = dot(stacked, hot[:, at])
        for j in range(step):
            p = b * step + j
            part = got[p, chans : chans + AUX, :].astype(F32)[0:1, :]
            total = jnp.zeros((chans, wide), F32)
            for h in range(parts):
                total = jnp.where(
                    part == h + 1.0,
                    y[h * chans : (h + 1) * chans, j * wide : (j + 1) * wide],
                    total,
                )
            back[p] = total.astype(BF)
        return carry

    lax.fori_loop(0, peers // step, one, 0, unroll=2)


def coarse_body(got, weight, weight_t, bias, back, grads, hot, masked, **sizes):
    coarse_hot(got, hot, masked, **sizes)
    low, top = coarse_totals(hot, masked, sizes["chans"], sizes["parts"])
    out, behind = coarse_math(low, top, weight, weight_t, bias, grads)
    coarse_gather(back, got, hot, out, behind, **sizes)


def totals_body(got, before, after, hot, masked, **sizes):
    chans = sizes["chans"]
    coarse_hot(got, hot, masked, **sizes)
    low, top = coarse_totals(hot, masked, chans, sizes["parts"])
    after[0:chans, :] = before[0:chans, :] + low
    after[chans : 2 * chans, :] = before[chans : 2 * chans, :] + top


def math_body(totals, weight, weight_t, bias, values, grads):
    chans = totals.shape[0] // 2
    out, behind = coarse_math(
        totals[0:chans, :], totals[chans : 2 * chans, :], weight, weight_t, bias, grads
    )
    values[0:chans, :] = out
    values[chans : 2 * chans, :] = behind


def gather_body(got, values, back, hot, **sizes):
    chans = sizes["chans"]
    coarse_hot(got, hot, None, **sizes)
    coarse_gather(
        back, got, hot, values[0:chans, :], values[chans : 2 * chans, :], **sizes
    )


def first_end_body(
    cols, tiles_h, f, g, f1, g1, up, down, inner, pool, mix_in, mix_out_t, bias,
    dest, rank, most, slot, owner,
    f2, g2, pre_in, hidden, merged_grad, sent, buffer, blocks, big, out, tiles, sems,
    *, chans, count, nonzero, compact, peers, cap, go, rows
):
    ready = fetched(tiles_h, tiles, sems, count, nonzero, compact)
    second_terms(
        cols, tiles, f, g, f1, up, down, inner, blocks, f2, g2, chans, count, nonzero, ready,
        compact,
    )

    def one(k):
        at = lanes(k)
        w = pool[:, at]
        pre = dot(mix_in[...], jnp.concatenate([f[:, at], f1[:, at], f2[:, at]], axis=0)) + bias[...]
        pre_in[:, at] = pre
        h = (pre * jax.nn.sigmoid(pre)).astype(BF)
        hidden[:, at] = h
        m = dot(mix_out_t[...], jnp.concatenate([g[:, at], g1[:, at], g2[:, at]], axis=0)).astype(BF)
        merged_grad[:, at] = m
        sent[0:chans, at] = (w * h.astype(F32)).astype(BF)
        sent[chans : 2 * chans, at] = (w * m.astype(F32)).astype(BF)

    each(count, one, compact)
    share = rows // 4 // peers
    index = owner[...] * share + slot[...] // peers
    part = index // LANES
    row = lax.broadcasted_iota(I32, (PAD, rows), 0)
    sent[2 * chans : 2 * chans + PAD, :] = (
        jnp.where(row == 0, part + 1, jnp.where(row == 1, index - part * LANES, 0))
        .astype(F32)
        .astype(BF)
    )
    needed = jnp.ceil(most[0:1, 0:1] * (1.0 / cap))
    pack_into(
        buffer, big, out, sent, dest[...], rank[...], needed, 0,
        chans=chans, peers=peers, cap=cap, go=go, rows=rows,
    )


def second_start_body(
    cols, tiles_h, lifted, hidden, merged_grad, pre_in, pool,
    merged, pre_grad, up, down, inner, ext, tiles, sems,
    *, chans, count, nonzero, compact
):
    ready = fetched(tiles_h, tiles, sems, count, nonzero, compact)

    def one(k):
        at = lanes(k)
        w = pool[:, at]
        merged[:, at] = (
            hidden[:, at].astype(F32) + w * lifted[0:chans, at].astype(F32)
        ).astype(BF)
        hidden_grad = merged_grad[:, at].astype(F32) + w * lifted[chans : 2 * chans, at].astype(F32)
        pre_grad[:, at] = (hidden_grad * slope(pre_in[:, at])).astype(BF)

    each(count, one, compact)

    def grad_of(k):
        ready(k)
        return tile(pre_grad, k)

    add_transposed(cols, tiles, grad_of, ext, count, nonzero, compact)
    write_sends(up, down, tile(merged, 0), tile(merged, count - 1), ext, chans, count)

    def one(k):
        inner[:, lanes(k)] = ext[k + 1]

    each(count, one, compact)


def weights_body(merged, pre_grad, f, f1, f2, g, g1, g2, mid, most, local, *, chans, cap):
    p, m = pre_grad[...], merged[...]
    gin = [dot_nt(p, t[...]) for t in (f, f1, f2)]
    gout = [dot_nt(t[...], m) for t in (g, g1, g2)]
    local[0:chans, :] = jnp.concatenate(gin + [mid[0:chans, :]], axis=1)
    total = dot_nt(jnp.ones(p.shape, BF), p)
    row = lax.broadcasted_iota(I32, (chans, chans), 0)
    sums = jnp.where(row == 0, total, mid[chans : 2 * chans, :])
    over = jnp.where(most[0:1, 0:1] > cap, 1.0, 0.0)
    sums = jnp.where(row == 2, over, sums)
    local[chans : 2 * chans, :] = jnp.concatenate(gout + [sums], axis=1)


def second_end_body(
    cols, tiles_h, f, g, f1, g1, up, down, inner, mix_out, mix_in_t,
    result, input_grad, f2, g2, blocks, tiles, sems,
    *, chans, count, nonzero, compact
):
    ready = fetched(tiles_h, tiles, sems, count, nonzero, compact)
    second_terms(
        cols, tiles, f, g, f1, up, down, inner, blocks, f2, g2, chans, count, nonzero, ready,
        compact,
    )

    def one(k):
        at = lanes(k)
        terms = jnp.concatenate([f[:, at], f1[:, at], f2[:, at]], axis=0)
        result[:, at] = dot(mix_out[...], terms).astype(BF)
        terms = jnp.concatenate([g[:, at], g1[:, at], g2[:, at]], axis=0)
        input_grad[:, at] = dot(mix_in_t[...], terms).astype(BF)

    each(count, one, compact)


def last_body(total, weights, biases, *, chans, factor):
    for k in range(7):
        low = k // 4 * chans
        at = slice(k % 4 * chans, (k % 4 + 1) * chans)
        weights[k] = total[low : low + chans, at] * factor
    biases[...] = total[chans : chans + 2, 3 * chans : 4 * chans] * factor


def spread(values, axes):
    peers = lax.axis_size(axes)
    return lax.all_to_all(
        jnp.broadcast_to(values[None], (peers, *values.shape)), axes, 0, 0, tiled=True
    )


def summed_everywhere(local):
    regions = lax.axis_size("region")
    parts = local.reshape(regions, -1, LANES)
    mine = lax.all_to_all(parts, "region", 0, 0, tiled=True)
    mine = jnp.sum(mine, axis=0)
    mine = spread(mine, ("geo", "sub"))
    mine = jnp.sum(mine, axis=0)
    return spread(mine, "region").reshape(local.shape)


def exchanged(buffer):
    return lax.all_to_all(buffer, LINE, 0, 0, tiled=True)


def on_device(*arrays):
    result, input_grad, weights, biases, over = level(*arrays, several=False)

    def again(carry):
        return (*level(*arrays, several=True)[:4], jnp.zeros_like(over))

    done = lax.while_loop(
        lambda carry: carry[4] > 0.5, again, (result, input_grad, weights, biases, over)
    )
    return done[0][None], done[1][None], done[2], done[3]


def level(
    features,
    lap_tiles,
    tile_cols,
    coarse_owner,
    coarse_slot,
    pool_weight,
    weight_in,
    weight_mid,
    weight_out,
    biases,
    out_grad,
    *,
    several,
):
    chans, rows = features.shape[1:]
    count, nonzero = lap_tiles.shape[1:3]
    peers = lax.axis_size(LINE)
    cap = 2 * rows // peers
    go = max(1, 256 // cap)
    coarse_rows = rows // 4
    parts = coarse_rows // LANES
    f, g = features[0], out_grad[0]
    tiles = lap_tiles[0].reshape(count * nonzero, LANES, LANES)
    cols = tile_cols[0]
    owner = coarse_owner[0].reshape(1, rows)
    slot = coarse_slot
    pool = pool_weight
    side = lambda w: jnp.concatenate([w[k] for k in range(3)], axis=1)
    side_t = lambda w: jnp.concatenate([w[k].T for k in range(3)], axis=1)
    line = dict(chans=chans, count=count, nonzero=nonzero, compact=several)
    ways = dict(chans=chans, peers=peers, cap=cap, go=go, rows=rows)
    sizes = dict(chans=chans, peers=peers, cap=cap, parts=parts)
    full = (chans, rows)
    halo = (2 * chans, LANES)
    ext = pltpu.VMEM((count + 2, chans, LANES), F32)
    blocks = pltpu.VMEM((count + 2, chans, LANES), BF)
    work = 2 * chans * rows * nonzero * LANES
    chunk = (peers, chans + AUX, 2 * cap)
    reply = (peers, chans, 2 * cap)
    hot_s = pltpu.VMEM((2 * LANES, peers * 2 * cap), BF)
    masked_s = pltpu.VMEM((parts * chans, peers * 2 * cap), BF)
    tall = peers // go * (2 * chans + PAD)
    pack_s = [pltpu.VMEM((tall, rows), BF), pltpu.VMEM((tall, go * cap), F32)]
    lift_s = [
        pltpu.VMEM((peers // go * 2 * chans, go * cap), BF),
        pltpu.VMEM((go * cap, rows), BF),
    ]
    store = [pltpu.VMEM(tiles.shape, BF), pltpu.SemaphoreType.DMA((4,))]
    bias_mid = biases[1][:, None]
    weight_mid_t = weight_mid.T

    def passed(up, down):
        up = shifted(up, 1)
        down = shifted(down, -1)
        return up, down

    def middle(field, up, down, inner):
        return call(
            functools.partial(middle_body, **line),
            [(full, BF), (full, BF), (halo, BF), (halo, BF), (full, F32)],
            [blocks, ext, *store],
            (cols, tiles, field, up, down, inner),
            smem=1,
            far=(1,),
            flops=2 * work,
        )

    up, down, inner = call(
        functools.partial(start_body, **line),
        [(halo, BF), (halo, BF), (full, F32)],
        [
            ext,
            pltpu.VMEM(tiles.shape, BF),
            pltpu.VMEM((2, chans, LANES), BF),
            pltpu.VMEM(full, BF),
            pltpu.SemaphoreType.DMA((7,)),
        ],
        (cols, tiles, f, g),
        smem=1,
        flops=work,
        far=(1, 2, 3),
        limit=START_LIMIT,
    )
    up, down = passed(up, down)
    dest, rank, most = call(
        functools.partial(place_body, peers=peers, rows=rows),
        [((1, rows), I32), ((1, rows), I32), ((AUX, LANES), F32)],
        [],
        (owner, slot),
        flops=2 * work,
    )
    f1, g1, up, down, inner = middle(f, up, down, inner)
    up, down = passed(up, down)
    f2, g2, pre_in, hidden, merged_grad, sent, buffer = call(
        functools.partial(first_end_body, **line, peers=peers, cap=cap, go=go, rows=rows),
        [
            (full, BF),
            (full, BF),
            (full, F32),
            (full, BF),
            (full, BF),
            ((2 * chans + PAD, rows), BF),
            (chunk, BF),
        ],
        [blocks, *pack_s, *store],
        (
            cols, tiles, f, g, f1, g1, up, down, inner, pool, side(weight_in), side_t(weight_out),
            biases[0][:, None], dest, rank, most, slot, owner,
        ),
        smem=1,
        flops=4 * work,
        limit=32,
        far=(1,),
    )
    got = exchanged(buffer)

    def unpacked(back, step):
        return call(
            functools.partial(unpack_body, **ways),
            [((2 * chans, rows), BF)],
            lift_s,
            (step, back, dest, rank),
            smem=1,
        )[0]

    def received(step):
        return exchanged(
            call(
                functools.partial(pack_body, **ways),
                [(chunk, BF)],
                pack_s,
                (step.reshape(1), sent, dest, rank, most),
                smem=1,
                limit=32,
            )[0]
        )

    def add(step, totals):
        return call(
            functools.partial(totals_body, **sizes),
            [((2 * chans, coarse_rows), F32)],
            [hot_s, masked_s],
            (received(step), totals),
            limit=32,
        )[0]

    if several:
        rounds = jnp.max(got[:, chans + 2, 0].astype(F32)).astype(I32)
        totals = lax.fori_loop(0, rounds, add, jnp.zeros((2 * chans, coarse_rows), F32))
        values, mid = call(
            math_body,
            [((2 * chans, coarse_rows), BF), ((2 * chans, chans), F32)],
            [],
            (totals, weight_mid, weight_mid_t, bias_mid),
        )

        def fetch(step, lifted):
            back = call(
                functools.partial(gather_body, **sizes),
                [(reply, BF)],
                [hot_s],
                (received(step), values),
                limit=32,
            )[0]
            return lifted + unpacked(exchanged(back), step.reshape(1))

        lifted = lax.fori_loop(0, rounds, fetch, jnp.zeros((2 * chans, rows), BF))
    else:
        back, mid = call(
            functools.partial(coarse_body, **sizes),
            [(reply, BF), ((2 * chans, chans), F32)],
            [hot_s, masked_s],
            (got, weight_mid, weight_mid_t, bias_mid),
            limit=32,
        )
        lifted = unpacked(exchanged(back), jnp.zeros((1,), I32))

    merged, pre_grad, up, down, inner = call(
        functools.partial(second_start_body, **line),
        [(full, BF), (full, BF), (halo, BF), (halo, BF), (full, F32)],
        [ext, *store],
        (cols, tiles, lifted, hidden, merged_grad, pre_in, pool),
        smem=1,
        far=(1,),
        flops=work,
    )
    up, down = passed(up, down)
    local = call(
        functools.partial(weights_body, chans=chans, cap=cap),
        [((2 * chans, LANES), F32)],
        [],
        (merged, pre_grad, f, f1, f2, g, g1, g2, mid, most),
        flops=work,
    )[0]
    m1, p1, up, down, inner = middle(merged, up, down, inner)
    up, down = passed(up, down)
    result, input_grad = call(
        functools.partial(second_end_body, **line),
        [(full, BF), (full, BF)],
        [pltpu.VMEM(full, BF), pltpu.VMEM(full, BF), blocks, *store],
        (
            cols, tiles, merged, pre_grad, m1, p1, up, down, inner,
            side(weight_out), side_t(weight_in),
        ),
        smem=1,
        flops=2 * work,
        far=(1,),
    )
    factor = 1.0 / math.sqrt(lax.axis_size("geo") * rows * peers)
    summed = summed_everywhere(local)
    sum_weights, sum_biases = call(
        functools.partial(last_body, chans=chans, factor=factor),
        [((7, chans, chans), F32), ((2, chans), F32)],
        [],
        (summed,),
    )
    return result, input_grad, sum_weights, sum_biases, summed[chans + 2, 3 * chans]


def solution(mesh):
    line = ("region", "sub")
    in_specs = (
        P("geo", None, line),
        P("geo", line, None, None, None),
        P("geo", line, None),
        P("geo", line, None),
        P("geo", line),
        P("geo", line),
        P(),
        P(),
        P(),
        P(),
        P("geo", None, line),
    )
    out_specs = (P("geo", None, line), P("geo", None, line), P(), P())
    return jax.shard_map(
        on_device, mesh=mesh, in_specs=in_specs, out_specs=out_specs, check_vma=False
    )
```

```python
import functools
import math

import jax
import jax.numpy as jnp
from jax import lax
from jax.experimental import pallas as pl
from jax.experimental.pallas import tpu as pltpu
from jax.sharding import PartitionSpec as P


LINE = ("region", "sub")
BF = jnp.bfloat16
F32 = jnp.float32
I32 = jnp.int32
LANES = 128
AUX = 8
START_LIMIT = 16
PAD = 16

VM = pl.BlockSpec(memory_space=pltpu.VMEM)
SM = pl.BlockSpec(memory_space=pltpu.SMEM)


def call(body, outs, scratch, args, smem=0, flops=0, limit=24, far=()):
    specs = [SM] * smem + [VM] * (len(args) - smem)
    for i in far:
        specs[i] = pl.BlockSpec(memory_space=pl.ANY)
    moved = sum(a.size * a.dtype.itemsize for a in args)
    return pl.pallas_call(
        body,
        out_shape=tuple(jax.ShapeDtypeStruct(s, d) for s, d in outs),
        in_specs=specs,
        out_specs=tuple(VM for _ in outs),
        scratch_shapes=scratch,
        cost_estimate=pl.CostEstimate(flops=flops, bytes_accessed=moved, transcendentals=0),
        compiler_params=pltpu.CompilerParams(vmem_limit_bytes=limit << 20),
    )(*args)


def dot(a, b):
    return jnp.dot(a, b, preferred_element_type=F32)


def dot_nt(a, b):
    return lax.dot_general(a, b, (((1,), (1,)), ((), ())), preferred_element_type=F32)


def lanes(k):
    if isinstance(k, int):
        return slice(k * LANES, (k + 1) * LANES)
    return pl.ds(pl.multiple_of(k * LANES, LANES), LANES)


def tile(ref, k):
    return ref[:, lanes(k)]


def each(count, one, compact):
    if not compact:
        for k in range(count):
            one(k)
        return

    def body(k, carry):
        one(k)
        return carry

    lax.fori_loop(0, count, body, 0)


def shifted(value, by):
    peers = lax.axis_size(LINE)
    pairs = [(i, i + by) for i in range(peers) if 0 <= i + by < peers]
    return lax.ppermute(value, LINE, pairs)


def add_transposed(cols, tiles, grad_of, ext, count, nonzero, compact):
    ext[...] = jnp.zeros_like(ext)

    def one(k):
        y = dot_nt(grad_of(k), row_tiles(tiles, k, nonzero))
        for n in range(nonzero):
            ext[cols[k, n]] += y[:, n * LANES : (n + 1) * LANES]

    each(count, one, compact)


def row_tiles(tiles, k, nonzero):
    return tiles[pl.ds(k * nonzero, nonzero)].reshape(nonzero * LANES, LANES)


def row_product(cols, tiles, blocks, k, nonzero):
    picked = [blocks[cols[k, n]] for n in range(nonzero)]
    return dot(jnp.concatenate(picked, axis=1), row_tiles(tiles, k, nonzero))


def fill_blocks(blocks, field, up, down, chans, count, compact):
    blocks[0] = up[0:chans, :]
    blocks[count + 1] = down[0:chans, :]

    def one(k):
        blocks[k + 1] = tile(field, k)

    each(count, one, compact)


def write_sends(up, down, first, last, ext, chans, count):
    up[0:chans, :] = last
    up[chans : 2 * chans, :] = ext[count + 1].astype(BF)
    down[0:chans, :] = first
    down[chans : 2 * chans, :] = ext[0].astype(BF)


def inner_tile(inner, up, down, k, chans, count):
    value = tile(inner, k)
    if not isinstance(k, int):
        first = jnp.where(k == 0, 1.0, 0.0)
        last = jnp.where(k == count - 1, 1.0, 0.0)
        value = value + first * up[chans : 2 * chans, :].astype(F32)
        return value + last * down[chans : 2 * chans, :].astype(F32)
    if k == 0:
        value = value + up[chans : 2 * chans, :].astype(F32)
    if k == count - 1:
        value = value + down[chans : 2 * chans, :].astype(F32)
    return value


def start_body(
    cols, tiles_h, f, g, up, down, inner, tiles, ext, sems, *, chans, count, nonzero, compact
):
    pieces = 4 if count % 4 == 0 else 1
    size = count // pieces
    copies = []
    for i in range(pieces):
        at = slice(i * size * nonzero, (i + 1) * size * nonzero)
        copies.append(pltpu.make_async_copy(tiles_h.at[at], tiles.at[at], sems.at[i]))
        copies[-1].start()
    if compact:
        for c in copies:
            c.wait()

    def grad_of(k):
        if not compact and k % size == 0:
            copies[k // size].wait()
        return tile(g, k)

    add_transposed(cols, tiles, grad_of, ext, count, nonzero, compact)
    write_sends(up, down, tile(f, 0), tile(f, count - 1), ext, chans, count)

    def one(k):
        inner[:, lanes(k)] = ext[k + 1]

    each(count, one, compact)


def middle_body(
    cols, tiles, f, up, down, inner, f1, g1, up2, down2, inner2, blocks, ext,
    *, chans, count, nonzero, compact
):
    fill_blocks(blocks, f, up, down, chans, count, compact)

    def one(k):
        g1[:, lanes(k)] = inner_tile(inner, up, down, k, chans, count).astype(BF)

    each(count, one, compact)

    def one(k):
        f1[:, lanes(k)] = row_product(cols, tiles, blocks, k, nonzero).astype(BF)

    each(count, one, compact)
    add_transposed(cols, tiles, lambda k: tile(g1, k), ext, count, nonzero, compact)
    write_sends(up2, down2, tile(f1, 0), tile(f1, count - 1), ext, chans, count)

    def one(k):
        inner2[:, lanes(k)] = ext[k + 1]

    each(count, one, compact)


def second_terms(
    cols, tiles, f, g, f1, up, down, inner, blocks, f2, g2, chans, count, nonzero, compact
):
    fill_blocks(blocks, f1, up, down, chans, count, compact)

    def one(k):
        at = lanes(k)
        y = row_product(cols, tiles, blocks, k, nonzero)
        f2[:, at] = (2.0 * y - f[:, at].astype(F32)).astype(BF)
        z = inner_tile(inner, up, down, k, chans, count)
        g2[:, at] = (2.0 * z - g[:, at].astype(F32)).astype(BF)

    each(count, one, compact)


def place_body(owner, slot, dest, rank, most, *, peers, rows):
    d = owner[...] + slot[...]
    d = d - (d // peers) * peers
    dest[...] = d
    hot = lax.broadcasted_iota(I32, (peers, rows), 0) == d
    hot = jnp.where(hot, 1.0, 0.0).astype(F32)
    a = lax.broadcasted_iota(I32, (LANES, LANES), 0)
    b = lax.broadcasted_iota(I32, (LANES, LANES), 1)
    before = jnp.where(a < b, 1.0, 0.0).astype(BF)
    carry = jnp.zeros((peers, 1), F32)
    for k in range(rows // LANES):
        h = hot[:, k * LANES : (k + 1) * LANES]
        c = dot(h.astype(BF), before) + carry
        rank[:, k * LANES : (k + 1) * LANES] = jnp.sum(h * c, axis=0, keepdims=True).astype(I32)
        carry = carry + jnp.sum(h, axis=1, keepdims=True)
    most[...] = jnp.broadcast_to(jnp.max(carry, axis=0, keepdims=True), (AUX, LANES))


def slot_hot(dest, rank, step, cap, go, rows):
    at = rank - step * cap
    inside = (at >= 0) & (at < cap)
    col = jnp.where(inside, (dest - (dest // go) * go) * cap + at, -1)
    hot = lax.broadcasted_iota(I32, (go * cap, rows), 0) == col
    return jnp.where(hot, 1.0, 0.0).astype(BF)


def merge_halves(low, high, odd, cap):
    if cap == LANES // 2:
        left = lax.broadcasted_iota(I32, low.shape, 1) < cap
        if odd:
            return jnp.where(left, pltpu.roll(low, cap, 1), high)
        return jnp.where(left, low, pltpu.roll(high, cap, 1))
    at = slice(cap, 2 * cap) if odd else slice(0, cap)
    return jnp.concatenate([low[:, at], high[:, at]], axis=1)


def pack_into(
    buffer, big, out, sent, dest, rank, most, step, *, chans, peers, cap, go, rows, compact
):
    unroll = 1 if compact else peers // go
    high = 2 * chans + PAD
    group = dest // go

    def mask(g, carry):
        here = jnp.where(group == g, 1.0, 0.0).astype(BF)
        big[pl.ds(pl.multiple_of(g * high, high), high), :] = sent[...] * here
        return carry

    lax.fori_loop(0, peers // go, mask, 0, unroll=unroll)
    out[...] = dot_nt(big[...], slot_hot(dest, rank, step, cap, go, rows))
    row = lax.broadcasted_iota(I32, (AUX, 2 * cap), 0)
    lane = lax.broadcasted_iota(I32, (AUX, 2 * cap), 1)
    extra = jnp.where((row == 1) & (lane >= cap), float(LANES), 0.0)
    extra = extra + jnp.where(row == 2, most, 0.0)

    def place(g, carry):
        part = out[pl.ds(pl.multiple_of(g * high, high), high), :]
        for o in range(go):
            pair = o // 2 * 2 * cap
            near = jnp.concatenate([part] * 2, axis=1) if go == 1 else part[:, pair : pair + 2 * cap]
            odd = o % 2 == 1
            p = g * go + o
            body = merge_halves(near[0:chans], near[chans : 2 * chans], odd, cap)
            buffer[p, 0:chans, :] = body.astype(BF)
            aux = near[2 * chans : 2 * chans + AUX]
            buffer[p, chans : chans + AUX, :] = (merge_halves(aux, aux, odd, cap) + extra).astype(BF)
        return carry

    lax.fori_loop(0, peers // go, place, 0, unroll=unroll)


def pack_body(step, sent, dest, rank, most, buffer, big, out, *, cap, **sizes):
    needed = jnp.ceil(most[0:1, 0:1] * (1.0 / cap))
    pack_into(buffer, big, out, sent, dest[...], rank[...], needed, step[0], cap=cap, **sizes)


def unpack_body(
    step, back, dest, rank, lifted, big, hot, *, chans, peers, cap, go, rows, compact
):
    unroll = 1 if compact else peers // go
    hot[...] = slot_hot(dest[...], rank[...], step[0], cap, go, rows)
    high = 2 * chans

    def gather(g, carry):
        rows_low = pl.ds(pl.multiple_of(g * high, high), chans)
        rows_top = pl.ds(pl.multiple_of(g * high + chans, chans), chans)
        for o in range(0, go, 2):
            a = back[g * go + o].astype(F32)
            if go == 1:
                low, top = a[:, 0:cap], a[:, cap : 2 * cap]
                at = slice(0, cap)
            else:
                b = back[g * go + o + 1].astype(F32)
                at = slice(o * cap, (o + 2) * cap)
                if cap == LANES // 2:
                    low, top = merge_halves(a, b, False, cap), merge_halves(a, b, True, cap)
                else:
                    low = jnp.concatenate([a[:, 0:cap], b[:, 0:cap]], axis=1)
                    top = jnp.concatenate([a[:, cap:], b[:, cap:]], axis=1)
            big[rows_low, at] = low.astype(BF)
            big[rows_top, at] = top.astype(BF)
        return carry

    lax.fori_loop(0, peers // go, gather, 0, unroll=unroll)
    width = min(256, rows)

    def select(w, carry):
        at = pl.ds(pl.multiple_of(w * width, width), width)
        y = dot(big[...], hot[:, at])
        group = dest[:, at] // go
        total = jnp.zeros((high, width), F32)
        for g in range(peers // go):
            total = jnp.where(group == g, y[g * high : (g + 1) * high], total)
        lifted[:, at] = total.astype(BF)
        return carry

    lax.fori_loop(0, rows // width, select, 0, unroll=1 if compact else rows // width)


def coarse_hot(got, hot, masked, *, chans, peers, cap, parts):
    wide = 2 * cap

    def one(p, carry):
        aux = got[p, chans : chans + AUX, :].astype(F32)
        at = pl.ds(pl.multiple_of(p * wide, wide), wide)
        code = aux[1:2, :].astype(I32)
        q = lax.broadcasted_iota(I32, (2 * LANES, wide), 0)
        hot[:, at] = jnp.where(q == code, 1.0, 0.0).astype(BF)
        if masked is not None:
            body = got[p, 0:chans, :].astype(F32)
            for h in range(parts):
                masked[h * chans : (h + 1) * chans, at] = jnp.where(
                    aux[0:1, :] == h + 1.0, body, 0.0
                ).astype(BF)
        return carry

    lax.fori_loop(0, peers, one, 0, unroll=4)


def coarse_totals(hot, masked, chans, parts):
    acc = dot_nt(masked[...], hot[...])
    split = [acc[h * chans : (h + 1) * chans] for h in range(parts)]
    low = jnp.concatenate([s[:, 0:LANES] for s in split], axis=1)
    top = jnp.concatenate([s[:, LANES:] for s in split], axis=1)
    return low, top


def slope(value):
    sig = jax.nn.sigmoid(value)
    return sig * (1.0 + value * (1.0 - sig))


def coarse_math(coarse_sum, coarse_grad, weight, weight_t, bias, grads):
    coarse = coarse_sum.astype(BF)
    pre = dot(weight[...], coarse) + bias[...]
    out = (pre * jax.nn.sigmoid(pre)).astype(BF)
    mid_grad = (coarse_grad * slope(pre)).astype(BF)
    chans = pre.shape[0]
    grads[0:chans, :] = dot_nt(mid_grad, coarse)
    ones = jnp.ones((chans, mid_grad.shape[1]), BF)
    grads[chans : 2 * chans, :] = dot_nt(ones, mid_grad)
    return out, dot(weight_t[...], mid_grad).astype(BF)


def coarse_gather(back, got, hot, out, behind, *, chans, peers, cap, parts):
    wide = 2 * cap
    stacked = [
        jnp.concatenate(
            [out[:, h * LANES : (h + 1) * LANES], behind[:, h * LANES : (h + 1) * LANES]], axis=1
        )
        for h in range(parts)
    ]
    stacked = jnp.concatenate(stacked, axis=0)
    step = max(1, 512 // wide)

    def one(b, carry):
        at = pl.ds(pl.multiple_of(b * step * wide, step * wide), step * wide)
        y = dot(stacked, hot[:, at])
        for j in range(step):
            p = b * step + j
            part = got[p, chans : chans + AUX, :].astype(F32)[0:1, :]
            total = jnp.zeros((chans, wide), F32)
            for h in range(parts):
                total = jnp.where(
                    part == h + 1.0,
                    y[h * chans : (h + 1) * chans, j * wide : (j + 1) * wide],
                    total,
                )
            back[p] = total.astype(BF)
        return carry

    lax.fori_loop(0, peers // step, one, 0, unroll=2)


def coarse_body(got, weight, weight_t, bias, back, grads, hot, masked, **sizes):
    coarse_hot(got, hot, masked, **sizes)
    low, top = coarse_totals(hot, masked, sizes["chans"], sizes["parts"])
    out, behind = coarse_math(low, top, weight, weight_t, bias, grads)
    coarse_gather(back, got, hot, out, behind, **sizes)


def totals_body(got, before, after, hot, masked, **sizes):
    chans = sizes["chans"]
    coarse_hot(got, hot, masked, **sizes)
    low, top = coarse_totals(hot, masked, chans, sizes["parts"])
    after[0:chans, :] = before[0:chans, :] + low
    after[chans : 2 * chans, :] = before[chans : 2 * chans, :] + top


def math_body(totals, weight, weight_t, bias, values, grads):
    chans = totals.shape[0] // 2
    out, behind = coarse_math(
        totals[0:chans, :], totals[chans : 2 * chans, :], weight, weight_t, bias, grads
    )
    values[0:chans, :] = out
    values[chans : 2 * chans, :] = behind


def gather_body(got, values, back, hot, **sizes):
    chans = sizes["chans"]
    coarse_hot(got, hot, None, **sizes)
    coarse_gather(
        back, got, hot, values[0:chans, :], values[chans : 2 * chans, :], **sizes
    )


def mixed(mix, first, second, third, k):
    at = lanes(k)
    return dot(mix[...], jnp.concatenate([first[:, at], second[:, at], third[:, at]], axis=0))


def first_end_body(
    cols, tiles, f, g, f1, g1, up, down, inner, pool, mix_in, mix_out_t, bias,
    dest, rank, most, slot, owner,
    f2, g2, buffer, sent, blocks, big, out,
    *, chans, count, nonzero, compact, peers, cap, go, rows
):
    second_terms(
        cols, tiles, f, g, f1, up, down, inner, blocks, f2, g2, chans, count, nonzero, compact
    )

    def one(k):
        at = lanes(k)
        w = pool[:, at]
        pre = mixed(mix_in, f, f1, f2, k) + bias[...]
        h = (pre * jax.nn.sigmoid(pre)).astype(BF)
        m = mixed(mix_out_t, g, g1, g2, k).astype(BF)
        sent[0:chans, at] = (w * h.astype(F32)).astype(BF)
        sent[chans : 2 * chans, at] = (w * m.astype(F32)).astype(BF)

    each(count, one, compact)
    share = rows // 4 // peers
    index = owner[...] * share + slot[...] // peers
    part = index // LANES
    row = lax.broadcasted_iota(I32, (PAD, rows), 0)
    sent[2 * chans : 2 * chans + PAD, :] = (
        jnp.where(row == 0, part + 1, jnp.where(row == 1, index - part * LANES, 0))
        .astype(F32)
        .astype(BF)
    )
    needed = jnp.ceil(most[0:1, 0:1] * (1.0 / cap))
    pack_into(
        buffer, big, out, sent, dest[...], rank[...], needed, 0,
        chans=chans, peers=peers, cap=cap, go=go, rows=rows, compact=compact,
    )


def second_start_body(
    cols, tiles, lifted, f, f1, f2, g, g1, g2, pool, mix_in, mix_out_t, bias,
    merged, pre_grad, up, down, inner, ext,
    *, chans, count, nonzero, compact
):
    def fine(k):
        at = lanes(k)
        w = pool[:, at]
        pre = mixed(mix_in, f, f1, f2, k) + bias[...]
        sig = jax.nn.sigmoid(pre)
        h = (pre * sig).astype(BF)
        m = mixed(mix_out_t, g, g1, g2, k).astype(BF)
        merged[:, at] = (h.astype(F32) + w * lifted[0:chans, at].astype(F32)).astype(BF)
        hidden_grad = m.astype(F32) + w * lifted[chans : 2 * chans, at].astype(F32)
        pre_grad[:, at] = (hidden_grad * (sig * (1.0 + pre * (1.0 - sig)))).astype(BF)

    each(count, fine, compact)
    add_transposed(cols, tiles, lambda k: tile(pre_grad, k), ext, count, nonzero, compact)
    write_sends(up, down, tile(merged, 0), tile(merged, count - 1), ext, chans, count)

    def one(k):
        inner[:, lanes(k)] = ext[k + 1]

    each(count, one, compact)


def weights_body(merged, pre_grad, f, f1, f2, g, g1, g2, mid, most, local, *, chans, cap):
    p, m = pre_grad[...], merged[...]
    gin = [dot_nt(p, t[...]) for t in (f, f1, f2)]
    gout = [dot_nt(t[...], m) for t in (g, g1, g2)]
    local[0:chans, :] = jnp.concatenate(gin + [mid[0:chans, :]], axis=1)
    total = dot_nt(jnp.ones(p.shape, BF), p)
    row = lax.broadcasted_iota(I32, (chans, chans), 0)
    sums = jnp.where(row == 0, total, mid[chans : 2 * chans, :])
    over = jnp.where(most[0:1, 0:1] > cap, 1.0, 0.0)
    sums = jnp.where(row == 2, over, sums)
    local[chans : 2 * chans, :] = jnp.concatenate(gout + [sums], axis=1)


def second_end_body(
    cols, tiles, f, g, f1, g1, up, down, inner, mix_out, mix_in_t,
    result, input_grad, f2, g2, blocks,
    *, chans, count, nonzero, compact
):
    second_terms(
        cols, tiles, f, g, f1, up, down, inner, blocks, f2, g2, chans, count, nonzero, compact
    )

    def one(k):
        at = lanes(k)
        terms = jnp.concatenate([f[:, at], f1[:, at], f2[:, at]], axis=0)
        result[:, at] = dot(mix_out[...], terms).astype(BF)
        terms = jnp.concatenate([g[:, at], g1[:, at], g2[:, at]], axis=0)
        input_grad[:, at] = dot(mix_in_t[...], terms).astype(BF)

    each(count, one, compact)


def last_body(total, weights, biases, *, chans, factor):
    for k in range(7):
        low = k // 4 * chans
        at = slice(k % 4 * chans, (k % 4 + 1) * chans)
        weights[k] = total[low : low + chans, at] * factor
    biases[...] = total[chans : chans + 2, 3 * chans : 4 * chans] * factor


def spread(values, axes):
    peers = lax.axis_size(axes)
    return lax.all_to_all(
        jnp.broadcast_to(values[None], (peers, *values.shape)), axes, 0, 0, tiled=True
    )


def summed_everywhere(local):
    regions = lax.axis_size("region")
    parts = local.reshape(regions, -1, LANES)
    mine = lax.all_to_all(parts, "region", 0, 0, tiled=True)
    mine = jnp.sum(mine, axis=0)
    mine = spread(mine, ("geo", "sub"))
    mine = jnp.sum(mine, axis=0)
    return spread(mine, "region").reshape(local.shape)


def exchanged(buffer):
    return lax.all_to_all(buffer, LINE, 0, 0, tiled=True)


def on_device(*arrays):
    result, input_grad, weights, biases, over = level(*arrays, several=False)

    def again(carry):
        return (*level(*arrays, several=True)[:4], jnp.zeros_like(over))

    done = lax.while_loop(
        lambda carry: carry[4] > 0.5, again, (result, input_grad, weights, biases, over)
    )
    return done[0][None], done[1][None], done[2], done[3]


def level(
    features,
    lap_tiles,
    tile_cols,
    coarse_owner,
    coarse_slot,
    pool_weight,
    weight_in,
    weight_mid,
    weight_out,
    biases,
    out_grad,
    *,
    several,
):
    chans, rows = features.shape[1:]
    count, nonzero = lap_tiles.shape[1:3]
    peers = lax.axis_size(LINE)
    cap = 2 * rows // peers
    go = max(1, 256 // cap)
    coarse_rows = rows // 4
    parts = coarse_rows // LANES
    f, g = features[0], out_grad[0]
    tiles = lap_tiles[0].reshape(count * nonzero, LANES, LANES)
    cols = tile_cols[0]
    owner = coarse_owner[0].reshape(1, rows)
    slot = coarse_slot
    pool = pool_weight
    side = lambda w: jnp.concatenate([w[k] for k in range(3)], axis=1)
    side_t = lambda w: jnp.concatenate([w[k].T for k in range(3)], axis=1)
    line = dict(chans=chans, count=count, nonzero=nonzero, compact=several)
    ways = dict(chans=chans, peers=peers, cap=cap, go=go, rows=rows, compact=several)
    sizes = dict(chans=chans, peers=peers, cap=cap, parts=parts)
    full = (chans, rows)
    halo = (2 * chans, LANES)
    ext = pltpu.VMEM((count + 2, chans, LANES), F32)
    blocks = pltpu.VMEM((count + 2, chans, LANES), BF)
    work = 2 * chans * rows * nonzero * LANES
    chunk = (peers, chans + AUX, 2 * cap)
    reply = (peers, chans, 2 * cap)
    hot_s = pltpu.VMEM((2 * LANES, peers * 2 * cap), BF)
    masked_s = pltpu.VMEM((parts * chans, peers * 2 * cap), BF)
    tall = peers // go * (2 * chans + PAD)
    pack_s = [pltpu.VMEM((tall, rows), BF), pltpu.VMEM((tall, go * cap), F32)]
    lift_s = [
        pltpu.VMEM((peers // go * 2 * chans, go * cap), BF),
        pltpu.VMEM((go * cap, rows), BF),
    ]
    bias_mid = biases[1][:, None]
    weight_mid_t = weight_mid.T

    def passed(up, down):
        up = shifted(up, 1)
        down = shifted(down, -1)
        return up, down

    def middle(field, up, down, inner):
        return call(
            functools.partial(middle_body, **line),
            [(full, BF), (full, BF), (halo, BF), (halo, BF), (full, F32)],
            [blocks, ext],
            (cols, tiles, field, up, down, inner),
            smem=1,
            flops=2 * work,
        )

    up, down, inner, tiles = call(
        functools.partial(start_body, **line),
        [(halo, BF), (halo, BF), (full, F32), (tiles.shape, BF)],
        [ext, pltpu.SemaphoreType.DMA((4,))],
        (cols, tiles, f, g),
        smem=1,
        far=(1,),
        limit=START_LIMIT,
        flops=work,
    )
    up, down = passed(up, down)
    dest, rank, most = call(
        functools.partial(place_body, peers=peers, rows=rows),
        [((1, rows), I32), ((1, rows), I32), ((AUX, LANES), F32)],
        [],
        (owner, slot),
        flops=2 * work,
    )
    f1, g1, up, down, inner = middle(f, up, down, inner)
    up, down = passed(up, down)
    mixes = (side(weight_in), side_t(weight_out), biases[0][:, None])
    packed = (2 * chans + PAD, rows)
    ended = call(
        functools.partial(first_end_body, **line, peers=peers, cap=cap, go=go, rows=rows),
        [(full, BF), (full, BF), (chunk, BF)] + [(packed, BF)] * several,
        [pltpu.VMEM(packed, BF)] * (not several) + [blocks, *pack_s],
        (
            cols, tiles, f, g, f1, g1, up, down, inner, pool, *mixes,
            dest, rank, most, slot, owner,
        ),
        smem=1,
        flops=4 * work,
        limit=32,
    )
    f2, g2, buffer = ended[:3]
    sent = ended[-1]
    got = exchanged(buffer)

    def unpacked(back, step):
        return call(
            functools.partial(unpack_body, **ways),
            [((2 * chans, rows), BF)],
            lift_s,
            (step, back, dest, rank),
            smem=1,
        )[0]

    def received(step):
        return exchanged(
            call(
                functools.partial(pack_body, **ways),
                [(chunk, BF)],
                pack_s,
                (step.reshape(1), sent, dest, rank, most),
                smem=1,
                limit=32,
            )[0]
        )

    def add(step, totals):
        return call(
            functools.partial(totals_body, **sizes),
            [((2 * chans, coarse_rows), F32)],
            [hot_s, masked_s],
            (received(step), totals),
            limit=32,
        )[0]

    if several:
        rounds = jnp.max(got[:, chans + 2, 0].astype(F32)).astype(I32)
        totals = lax.fori_loop(0, rounds, add, jnp.zeros((2 * chans, coarse_rows), F32))
        values, mid = call(
            math_body,
            [((2 * chans, coarse_rows), BF), ((2 * chans, chans), F32)],
            [],
            (totals, weight_mid, weight_mid_t, bias_mid),
        )

        def fetch(step, lifted):
            back = call(
                functools.partial(gather_body, **sizes),
                [(reply, BF)],
                [hot_s],
                (received(step), values),
                limit=32,
            )[0]
            return lifted + unpacked(exchanged(back), step.reshape(1))

        lifted = lax.fori_loop(0, rounds, fetch, jnp.zeros((2 * chans, rows), BF))
    else:
        back, mid = call(
            functools.partial(coarse_body, **sizes),
            [(reply, BF), ((2 * chans, chans), F32)],
            [hot_s, masked_s],
            (got, weight_mid, weight_mid_t, bias_mid),
            limit=32,
        )
        lifted = unpacked(exchanged(back), jnp.zeros((1,), I32))

    merged, pre_grad, up, down, inner = call(
        functools.partial(second_start_body, **line),
        [(full, BF), (full, BF), (halo, BF), (halo, BF), (full, F32)],
        [ext],
        (cols, tiles, lifted, f, f1, f2, g, g1, g2, pool, *mixes),
        smem=1,
        flops=work,
    )
    up, down = passed(up, down)
    local = call(
        functools.partial(weights_body, chans=chans, cap=cap),
        [((2 * chans, LANES), F32)],
        [],
        (merged, pre_grad, f, f1, f2, g, g1, g2, mid, most),
        flops=work,
    )[0]
    m1, p1, up, down, inner = middle(merged, up, down, inner)
    up, down = passed(up, down)
    result, input_grad = call(
        functools.partial(second_end_body, **line),
        [(full, BF), (full, BF)],
        [pltpu.VMEM(full, BF), pltpu.VMEM(full, BF), blocks],
        (
            cols, tiles, merged, pre_grad, m1, p1, up, down, inner,
            side(weight_out), side_t(weight_in),
        ),
        smem=1,
        flops=2 * work,
    )
    factor = 1.0 / math.sqrt(lax.axis_size("geo") * rows * peers)
    summed = summed_everywhere(local)
    sum_weights, sum_biases = call(
        functools.partial(last_body, chans=chans, factor=factor),
        [((7, chans, chans), F32), ((2, chans), F32)],
        [],
        (summed,),
    )
    return result, input_grad, sum_weights, sum_biases, summed[chans + 2, 3 * chans]


def solution(mesh):
    line = ("region", "sub")
    in_specs = (
        P("geo", None, line),
        P("geo", line, None, None, None),
        P("geo", line, None),
        P("geo", line, None),
        P("geo", line),
        P("geo", line),
        P(),
        P(),
        P(),
        P(),
        P("geo", None, line),
    )
    out_specs = (P("geo", None, line), P("geo", None, line), P(), P())
    return jax.shard_map(
        on_device, mesh=mesh, in_specs=in_specs, out_specs=out_specs, check_vma=False
    )
```

```python
import functools
import math

import jax
import jax.numpy as jnp
from jax import lax
from jax.experimental import pallas as pl
from jax.experimental.pallas import tpu as pltpu
from jax.sharding import PartitionSpec as P


LINE = ("region", "sub")
BF = jnp.bfloat16
F32 = jnp.float32
I32 = jnp.int32
LANES = 128
AUX = 8
START_LIMIT = 16
PAD = 16

VM = pl.BlockSpec(memory_space=pltpu.VMEM)
SM = pl.BlockSpec(memory_space=pltpu.SMEM)


def call(body, outs, scratch, args, smem=0, flops=0, limit=24, far=(), smem_out=()):
    specs = [SM] * smem + [VM] * (len(args) - smem)
    for i in far:
        specs[i] = pl.BlockSpec(memory_space=pl.ANY)
    moved = sum(a.size * a.dtype.itemsize for a in args)
    return pl.pallas_call(
        body,
        out_shape=tuple(jax.ShapeDtypeStruct(s, d) for s, d in outs),
        in_specs=specs,
        out_specs=tuple(SM if i in smem_out else VM for i in range(len(outs))),
        scratch_shapes=scratch,
        cost_estimate=pl.CostEstimate(flops=flops, bytes_accessed=moved, transcendentals=0),
        compiler_params=pltpu.CompilerParams(vmem_limit_bytes=limit << 20),
    )(*args)


def dot(a, b):
    return jnp.dot(a, b, preferred_element_type=F32)


def dot_nt(a, b):
    return lax.dot_general(a, b, (((1,), (1,)), ((), ())), preferred_element_type=F32)


def lanes(k):
    if isinstance(k, int):
        return slice(k * LANES, (k + 1) * LANES)
    return pl.ds(pl.multiple_of(k * LANES, LANES), LANES)


def tile(ref, k):
    return ref[:, lanes(k)]


def each(count, one, compact):
    if not compact:
        for k in range(count):
            one(k)
        return

    def body(k, carry):
        one(k)
        return carry

    lax.fori_loop(0, count, body, 0)


def shifted(value, by):
    peers = lax.axis_size(LINE)
    pairs = [(i, i + by) for i in range(peers) if 0 <= i + by < peers]
    return lax.ppermute(value, LINE, pairs)


def add_transposed(cols, tiles, grad_of, ext, count, nonzero, compact):
    ext[...] = jnp.zeros_like(ext)

    def one(k):
        y = dot_nt(grad_of(k), row_tiles(tiles, k, nonzero))
        for n in range(nonzero):
            ext[cols[n, k]] += y[:, n * LANES : (n + 1) * LANES]

    each(count, one, compact)


def row_tiles(tiles, k, nonzero):
    return tiles[pl.ds(k * nonzero, nonzero)].reshape(nonzero * LANES, LANES)


def row_product(cols, tiles, blocks, k, nonzero):
    picked = [blocks[cols[n, k]] for n in range(nonzero)]
    return dot(jnp.concatenate(picked, axis=1), row_tiles(tiles, k, nonzero))


def fill_blocks(blocks, field, up, down, chans, count, compact):
    blocks[0] = up[0:chans, :]
    blocks[count + 1] = down[0:chans, :]

    def one(k):
        blocks[k + 1] = tile(field, k)

    each(count, one, compact)


def write_sends(up, down, first, last, ext, chans, count):
    up[0:chans, :] = last
    up[chans : 2 * chans, :] = ext[count + 1].astype(BF)
    down[0:chans, :] = first
    down[chans : 2 * chans, :] = ext[0].astype(BF)


def inner_tile(inner, up, down, k, chans, count):
    value = tile(inner, k)
    if not isinstance(k, int):
        first = jnp.where(k == 0, 1.0, 0.0)
        last = jnp.where(k == count - 1, 1.0, 0.0)
        value = value + first * up[chans : 2 * chans, :].astype(F32)
        return value + last * down[chans : 2 * chans, :].astype(F32)
    if k == 0:
        value = value + up[chans : 2 * chans, :].astype(F32)
    if k == count - 1:
        value = value + down[chans : 2 * chans, :].astype(F32)
    return value


def start_body(
    cols, tiles_h, f, g, up, down, inner, tiles, ext, sems, *, chans, count, nonzero, compact
):
    pieces = 4 if count % 4 == 0 else 1
    size = count // pieces
    copies = []
    for i in range(pieces):
        at = slice(i * size * nonzero, (i + 1) * size * nonzero)
        copies.append(pltpu.make_async_copy(tiles_h.at[at], tiles.at[at], sems.at[i]))
        copies[-1].start()
    if compact:
        for c in copies:
            c.wait()

    def grad_of(k):
        if not compact and k % size == 0:
            copies[k // size].wait()
        return tile(g, k)

    add_transposed(cols, tiles, grad_of, ext, count, nonzero, compact)
    write_sends(up, down, tile(f, 0), tile(f, count - 1), ext, chans, count)

    def one(k):
        inner[:, lanes(k)] = ext[k + 1]

    each(count, one, compact)


def middle_body(
    cols, tiles, f, up, down, inner, f1, g1, up2, down2, inner2, blocks, ext,
    *, chans, count, nonzero, compact
):
    fill_blocks(blocks, f, up, down, chans, count, compact)

    def one(k):
        g1[:, lanes(k)] = inner_tile(inner, up, down, k, chans, count).astype(BF)

    each(count, one, compact)

    def one(k):
        f1[:, lanes(k)] = row_product(cols, tiles, blocks, k, nonzero).astype(BF)

    each(count, one, compact)
    add_transposed(cols, tiles, lambda k: tile(g1, k), ext, count, nonzero, compact)
    write_sends(up2, down2, tile(f1, 0), tile(f1, count - 1), ext, chans, count)

    def one(k):
        inner2[:, lanes(k)] = ext[k + 1]

    each(count, one, compact)


def second_terms(
    cols, tiles, f, g, f1, up, down, inner, blocks, f2, g2, chans, count, nonzero, compact
):
    fill_blocks(blocks, f1, up, down, chans, count, compact)

    def one(k):
        at = lanes(k)
        y = row_product(cols, tiles, blocks, k, nonzero)
        f2[:, at] = (2.0 * y - f[:, at].astype(F32)).astype(BF)
        z = inner_tile(inner, up, down, k, chans, count)
        g2[:, at] = (2.0 * z - g[:, at].astype(F32)).astype(BF)

    each(count, one, compact)


def prepare_body(
    w_in, w_mid, w_out, biases, mix_in, mix_in_t, mix_out, mix_out_t, mid, mid_t, bias_in, bias_mid,
    *, chans
):
    flip = lambda w: w.astype(F32).T.astype(BF)
    for source, plain, turned in ((w_in, mix_in, mix_in_t), (w_out, mix_out, mix_out_t)):
        plain[...] = jnp.concatenate([source[k] for k in range(3)], axis=1)
        turned[...] = jnp.concatenate([flip(source[k]) for k in range(3)], axis=1)
    mid[...] = w_mid[...]
    mid_t[...] = flip(w_mid[...])
    same = lax.broadcasted_iota(I32, (chans, chans), 0) == lax.broadcasted_iota(I32, (chans, chans), 1)
    for row, column in ((0, bias_in), (1, bias_mid)):
        column[...] = jnp.sum(jnp.where(same, biases[row : row + 1, :], 0.0), axis=1, keepdims=True)


def place_body(owner, slot, dest, rank, most, *, peers, rows):
    d = owner[...] + slot[...]
    d = d - (d // peers) * peers
    dest[...] = d
    hot = lax.broadcasted_iota(I32, (peers, rows), 0) == d
    hot = jnp.where(hot, 1.0, 0.0).astype(F32)
    a = lax.broadcasted_iota(I32, (LANES, LANES), 0)
    b = lax.broadcasted_iota(I32, (LANES, LANES), 1)
    before = jnp.where(a < b, 1.0, 0.0).astype(BF)
    carry = jnp.zeros((peers, 1), F32)
    for k in range(rows // LANES):
        h = hot[:, k * LANES : (k + 1) * LANES]
        c = dot(h.astype(BF), before) + carry
        rank[:, k * LANES : (k + 1) * LANES] = jnp.sum(h * c, axis=0, keepdims=True).astype(I32)
        carry = carry + jnp.sum(h, axis=1, keepdims=True)
    most[...] = jnp.broadcast_to(jnp.max(carry, axis=0, keepdims=True), (AUX, LANES))


def slot_hot(dest, rank, step, cap, go, rows):
    at = rank - step * cap
    inside = (at >= 0) & (at < cap)
    col = jnp.where(inside, (dest - (dest // go) * go) * cap + at, -1)
    hot = lax.broadcasted_iota(I32, (go * cap, rows), 0) == col
    return jnp.where(hot, 1.0, 0.0).astype(BF)


def merge_halves(low, high, odd, cap):
    if cap == LANES // 2:
        left = lax.broadcasted_iota(I32, low.shape, 1) < cap
        if odd:
            return jnp.where(left, pltpu.roll(low, cap, 1), high)
        return jnp.where(left, low, pltpu.roll(high, cap, 1))
    at = slice(cap, 2 * cap) if odd else slice(0, cap)
    return jnp.concatenate([low[:, at], high[:, at]], axis=1)


def pack_into(
    buffer, big, out, sent, dest, rank, most, step, *, chans, peers, cap, go, rows, compact
):
    unroll = 1 if compact else peers // go
    high = 2 * chans + PAD
    group = dest // go

    def mask(g, carry):
        here = jnp.where(group == g, 1.0, 0.0).astype(BF)
        big[pl.ds(pl.multiple_of(g * high, high), high), :] = sent[...] * here
        return carry

    lax.fori_loop(0, peers // go, mask, 0, unroll=unroll)
    out[...] = dot_nt(big[...], slot_hot(dest, rank, step, cap, go, rows))
    row = lax.broadcasted_iota(I32, (AUX, 2 * cap), 0)
    lane = lax.broadcasted_iota(I32, (AUX, 2 * cap), 1)
    extra = jnp.where((row == 1) & (lane >= cap), float(LANES), 0.0)
    extra = extra + jnp.where(row == 2, most, 0.0)

    def place(g, carry):
        part = out[pl.ds(pl.multiple_of(g * high, high), high), :]
        for o in range(go):
            pair = o // 2 * 2 * cap
            near = jnp.concatenate([part] * 2, axis=1) if go == 1 else part[:, pair : pair + 2 * cap]
            odd = o % 2 == 1
            p = g * go + o
            body = merge_halves(near[0:chans], near[chans : 2 * chans], odd, cap)
            buffer[p, 0:chans, :] = body.astype(BF)
            aux = near[2 * chans : 2 * chans + AUX]
            buffer[p, chans : chans + AUX, :] = (merge_halves(aux, aux, odd, cap) + extra).astype(BF)
        return carry

    lax.fori_loop(0, peers // go, place, 0, unroll=unroll)


def pack_body(step, sent, dest, rank, most, buffer, big, out, *, cap, **sizes):
    needed = jnp.ceil(most[0:1, 0:1] * (1.0 / cap))
    pack_into(buffer, big, out, sent, dest[...], rank[...], needed, step[0], cap=cap, **sizes)


def unpack_body(
    step, back, dest, rank, lifted, big, hot, *, chans, peers, cap, go, rows, compact
):
    unroll = 1 if compact else peers // go
    hot[...] = slot_hot(dest[...], rank[...], step[0], cap, go, rows)
    high = 2 * chans

    def gather(g, carry):
        rows_low = pl.ds(pl.multiple_of(g * high, high), chans)
        rows_top = pl.ds(pl.multiple_of(g * high + chans, chans), chans)
        for o in range(0, go, 2):
            a = back[g * go + o].astype(F32)
            if go == 1:
                low, top = a[:, 0:cap], a[:, cap : 2 * cap]
                at = slice(0, cap)
            else:
                b = back[g * go + o + 1].astype(F32)
                at = slice(o * cap, (o + 2) * cap)
                if cap == LANES // 2:
                    low, top = merge_halves(a, b, False, cap), merge_halves(a, b, True, cap)
                else:
                    low = jnp.concatenate([a[:, 0:cap], b[:, 0:cap]], axis=1)
                    top = jnp.concatenate([a[:, cap:], b[:, cap:]], axis=1)
            big[rows_low, at] = low.astype(BF)
            big[rows_top, at] = top.astype(BF)
        return carry

    lax.fori_loop(0, peers // go, gather, 0, unroll=unroll)
    width = min(256, rows)

    def select(w, carry):
        at = pl.ds(pl.multiple_of(w * width, width), width)
        y = dot(big[...], hot[:, at])
        group = dest[:, at] // go
        total = jnp.zeros((high, width), F32)
        for g in range(peers // go):
            total = jnp.where(group == g, y[g * high : (g + 1) * high], total)
        lifted[:, at] = total.astype(BF)
        return carry

    lax.fori_loop(0, rows // width, select, 0, unroll=1 if compact else rows // width)


def coarse_hot(got, hot, masked, *, chans, peers, cap, parts):
    wide = 2 * cap

    def one(p, carry):
        aux = got[p, chans : chans + AUX, :].astype(F32)
        at = pl.ds(pl.multiple_of(p * wide, wide), wide)
        code = aux[1:2, :].astype(I32)
        q = lax.broadcasted_iota(I32, (2 * LANES, wide), 0)
        hot[:, at] = jnp.where(q == code, 1.0, 0.0).astype(BF)
        if masked is not None:
            body = got[p, 0:chans, :].astype(F32)
            for h in range(parts):
                masked[h * chans : (h + 1) * chans, at] = jnp.where(
                    aux[0:1, :] == h + 1.0, body, 0.0
                ).astype(BF)
        return carry

    lax.fori_loop(0, peers, one, 0, unroll=4)


def coarse_totals(hot, masked, chans, parts):
    acc = dot_nt(hot[...], masked[...]).T
    split = [acc[h * chans : (h + 1) * chans] for h in range(parts)]
    low = jnp.concatenate([s[:, 0:LANES] for s in split], axis=1)
    top = jnp.concatenate([s[:, LANES:] for s in split], axis=1)
    return low, top


def slope(value):
    sig = jax.nn.sigmoid(value)
    return sig * (1.0 + value * (1.0 - sig))


def coarse_math(coarse_sum, coarse_grad, weight, weight_t, bias, grads):
    coarse = coarse_sum.astype(BF)
    pre = dot(weight[...], coarse) + bias[...]
    out = (pre * jax.nn.sigmoid(pre)).astype(BF)
    mid_grad = (coarse_grad * slope(pre)).astype(BF)
    chans = pre.shape[0]
    grads[0:chans, :] = dot_nt(mid_grad, coarse)
    ones = jnp.ones((chans, mid_grad.shape[1]), BF)
    grads[chans : 2 * chans, :] = dot_nt(ones, mid_grad)
    return out, dot(weight_t[...], mid_grad).astype(BF)


def coarse_gather(back, got, hot, out, behind, *, chans, peers, cap, parts):
    wide = 2 * cap
    stacked = [
        jnp.concatenate(
            [out[:, h * LANES : (h + 1) * LANES], behind[:, h * LANES : (h + 1) * LANES]], axis=1
        )
        for h in range(parts)
    ]
    stacked = jnp.concatenate(stacked, axis=0)
    step = max(1, 512 // wide)

    def one(b, carry):
        at = pl.ds(pl.multiple_of(b * step * wide, step * wide), step * wide)
        y = dot(stacked, hot[:, at])
        for j in range(step):
            p = b * step + j
            part = got[p, chans : chans + AUX, :].astype(F32)[0:1, :]
            total = jnp.zeros((chans, wide), F32)
            for h in range(parts):
                total = jnp.where(
                    part == h + 1.0,
                    y[h * chans : (h + 1) * chans, j * wide : (j + 1) * wide],
                    total,
                )
            back[p] = total.astype(BF)
        return carry

    lax.fori_loop(0, peers // step, one, 0, unroll=2)


def coarse_body(got, weight, weight_t, bias, back, grads, hot, masked, **sizes):
    coarse_hot(got, hot, masked, **sizes)
    low, top = coarse_totals(hot, masked, sizes["chans"], sizes["parts"])
    out, behind = coarse_math(low, top, weight, weight_t, bias, grads)
    coarse_gather(back, got, hot, out, behind, **sizes)


def totals_body(got, before, after, hot, masked, **sizes):
    chans = sizes["chans"]
    coarse_hot(got, hot, masked, **sizes)
    low, top = coarse_totals(hot, masked, chans, sizes["parts"])
    after[0:chans, :] = before[0:chans, :] + low
    after[chans : 2 * chans, :] = before[chans : 2 * chans, :] + top


def math_body(totals, weight, weight_t, bias, values, grads):
    chans = totals.shape[0] // 2
    out, behind = coarse_math(
        totals[0:chans, :], totals[chans : 2 * chans, :], weight, weight_t, bias, grads
    )
    values[0:chans, :] = out
    values[chans : 2 * chans, :] = behind


def gather_body(got, values, back, hot, **sizes):
    chans = sizes["chans"]
    coarse_hot(got, hot, None, **sizes)
    coarse_gather(
        back, got, hot, values[0:chans, :], values[chans : 2 * chans, :], **sizes
    )


def mixed(mix, first, second, third, k):
    at = lanes(k)
    return dot(mix[...], jnp.concatenate([first[:, at], second[:, at], third[:, at]], axis=0))


def first_end_body(
    cols, tiles, f, g, f1, g1, up, down, inner, pool, mix_in, mix_out_t, bias,
    dest, rank, most, slot, owner,
    f2, g2, buffer, sent, blocks, big, out,
    *, chans, count, nonzero, compact, peers, cap, go, rows
):
    second_terms(
        cols, tiles, f, g, f1, up, down, inner, blocks, f2, g2, chans, count, nonzero, compact
    )

    def one(k):
        at = lanes(k)
        w = pool[:, at]
        pre = mixed(mix_in, f, f1, f2, k) + bias[...]
        h = (pre * jax.nn.sigmoid(pre)).astype(BF)
        m = mixed(mix_out_t, g, g1, g2, k).astype(BF)
        sent[0:chans, at] = (w * h.astype(F32)).astype(BF)
        sent[chans : 2 * chans, at] = (w * m.astype(F32)).astype(BF)

    each(count, one, compact)
    share = rows // 4 // peers
    index = owner[...] * share + slot[...] // peers
    part = index // LANES
    row = lax.broadcasted_iota(I32, (PAD, rows), 0)
    sent[2 * chans : 2 * chans + PAD, :] = (
        jnp.where(row == 0, part + 1, jnp.where(row == 1, index - part * LANES, 0))
        .astype(F32)
        .astype(BF)
    )
    needed = jnp.ceil(most[0:1, 0:1] * (1.0 / cap))
    pack_into(
        buffer, big, out, sent, dest[...], rank[...], needed, 0,
        chans=chans, peers=peers, cap=cap, go=go, rows=rows, compact=compact,
    )


def second_start_body(
    cols, tiles, lifted, f, f1, f2, g, g1, g2, pool, mix_in, mix_out_t, bias,
    merged, pre_grad, up, down, inner, ext,
    *, chans, count, nonzero, compact
):
    def fine(k):
        at = lanes(k)
        w = pool[:, at]
        pre = mixed(mix_in, f, f1, f2, k) + bias[...]
        sig = jax.nn.sigmoid(pre)
        h = (pre * sig).astype(BF)
        m = mixed(mix_out_t, g, g1, g2, k).astype(BF)
        merged[:, at] = (h.astype(F32) + w * lifted[0:chans, at].astype(F32)).astype(BF)
        hidden_grad = m.astype(F32) + w * lifted[chans : 2 * chans, at].astype(F32)
        pre_grad[:, at] = (hidden_grad * (sig * (1.0 + pre * (1.0 - sig)))).astype(BF)

    each(count, fine, compact)
    add_transposed(cols, tiles, lambda k: tile(pre_grad, k), ext, count, nonzero, compact)
    write_sends(up, down, tile(merged, 0), tile(merged, count - 1), ext, chans, count)

    def one(k):
        inner[:, lanes(k)] = ext[k + 1]

    each(count, one, compact)


def weights_body(merged, pre_grad, f, f1, f2, g, g1, g2, mid, most, local, *, chans, cap):
    p, m = pre_grad[...], merged[...]
    gin = [dot_nt(p, t[...]) for t in (f, f1, f2)]
    gout = [dot_nt(t[...], m) for t in (g, g1, g2)]
    total = dot_nt(jnp.ones(p.shape, BF), p)
    row = lax.broadcasted_iota(I32, (chans, chans), 0)
    sums = jnp.where(row == 0, total, mid[chans : 2 * chans, :])
    over = jnp.where(most[0:1, 0:1] > cap, 1.0, 0.0)
    sums = jnp.where(row == 2, over, sums)
    upper = jnp.concatenate(gin + [mid[0:chans, :]], axis=1).astype(BF)
    lower = jnp.concatenate(gout + [sums], axis=1).astype(BF)
    for i in range(local.shape[0]):
        local[i, 0:chans, :] = upper
        local[i, chans : 2 * chans, :] = lower


def second_end_body(
    cols, tiles, f, g, f1, g1, up, down, inner, mix_out, mix_in_t,
    result, input_grad, f2, g2, blocks,
    *, chans, count, nonzero, compact
):
    second_terms(
        cols, tiles, f, g, f1, up, down, inner, blocks, f2, g2, chans, count, nonzero, compact
    )

    def one(k):
        at = lanes(k)
        terms = jnp.concatenate([f[:, at], f1[:, at], f2[:, at]], axis=0)
        result[:, at] = dot(mix_out[...], terms).astype(BF)
        terms = jnp.concatenate([g[:, at], g1[:, at], g2[:, at]], axis=0)
        input_grad[:, at] = dot(mix_in_t[...], terms).astype(BF)

    each(count, one, compact)


def total_of(got):
    total = got[0].astype(F32)
    for i in range(1, got.shape[0]):
        total = total + got[i].astype(F32)
    return total


def relay_body(got, spread):
    total = total_of(got).astype(BF)
    for i in range(spread.shape[0]):
        spread[i] = total


def last_body(got, weights, biases, over, total, *, chans, factor):
    total[...] = total_of(got)
    over[0] = jnp.sum(total[chans + 2 : chans + 3, 3 * chans : 3 * chans + 1])
    for k in range(7):
        low = k // 4 * chans
        at = slice(k % 4 * chans, (k % 4 + 1) * chans)
        weights[k] = total[low : low + chans, at] * factor
    biases[...] = total[chans : chans + 2, 3 * chans : 4 * chans] * factor


def exchanged(buffer):
    return lax.all_to_all(buffer, LINE, 0, 0, tiled=True)


def on_device(*arrays):
    result, input_grad, weights, biases, over = level(*arrays, several=False)

    def again(carry):
        return (*level(*arrays, several=True)[:4], jnp.zeros_like(over))

    done = lax.while_loop(
        lambda carry: carry[4] > 0.5, again, (result, input_grad, weights, biases, over)
    )
    return done[0][None], done[1][None], done[2], done[3]


def level(
    features,
    lap_tiles,
    tile_cols,
    coarse_owner,
    coarse_slot,
    pool_weight,
    weight_in,
    weight_mid,
    weight_out,
    biases,
    out_grad,
    *,
    several,
):
    chans, rows = features.shape[1:]
    count, nonzero = lap_tiles.shape[1:3]
    peers = lax.axis_size(LINE)
    cap = 2 * rows // peers
    go = max(1, 256 // cap)
    coarse_rows = rows // 4
    parts = coarse_rows // LANES
    f, g = features[0], out_grad[0]
    tiles = lap_tiles[0].reshape(count * nonzero, LANES, LANES)
    cols = tile_cols[0].T
    owner = coarse_owner[0].reshape(1, rows)
    slot = coarse_slot
    pool = pool_weight
    line = dict(chans=chans, count=count, nonzero=nonzero, compact=several)
    ways = dict(chans=chans, peers=peers, cap=cap, go=go, rows=rows, compact=several)
    sizes = dict(chans=chans, peers=peers, cap=cap, parts=parts)
    full = (chans, rows)
    halo = (2 * chans, LANES)
    ext = pltpu.VMEM((count + 2, chans, LANES), F32)
    blocks = pltpu.VMEM((count + 2, chans, LANES), BF)
    work = 2 * chans * rows * nonzero * LANES
    chunk = (peers, chans + AUX, 2 * cap)
    reply = (peers, chans, 2 * cap)
    hot_s = pltpu.VMEM((2 * LANES, peers * 2 * cap), BF)
    masked_s = pltpu.VMEM((parts * chans, peers * 2 * cap), BF)
    tall = peers // go * (2 * chans + PAD)
    pack_s = [pltpu.VMEM((tall, rows), BF), pltpu.VMEM((tall, go * cap), F32)]
    lift_s = [
        pltpu.VMEM((peers // go * 2 * chans, go * cap), BF),
        pltpu.VMEM((go * cap, rows), BF),
    ]
    small = (chans, chans)
    wide = (chans, 3 * chans)
    mix_in, mix_in_t, mix_out, mix_out_t, mid_w, mid_t, bias_in, bias_mid = call(
        functools.partial(prepare_body, chans=chans),
        [(wide, BF)] * 4 + [(small, BF)] * 2 + [((chans, 1), F32)] * 2,
        [],
        (weight_in, weight_mid, weight_out, biases),
        flops=2 * work,
    )

    def passed(up, down):
        up = shifted(up, 1)
        down = shifted(down, -1)
        return up, down

    def middle(field, up, down, inner):
        return call(
            functools.partial(middle_body, **line),
            [(full, BF), (full, BF), (halo, BF), (halo, BF), (full, F32)],
            [blocks, ext],
            (cols, tiles, field, up, down, inner),
            smem=1,
            flops=2 * work,
        )

    up, down, inner, tiles = call(
        functools.partial(start_body, **line),
        [(halo, BF), (halo, BF), (full, F32), (tiles.shape, BF)],
        [ext, pltpu.SemaphoreType.DMA((4,))],
        (cols, tiles, f, g),
        smem=1,
        far=(1,),
        limit=START_LIMIT,
        flops=work,
    )
    up, down = passed(up, down)
    dest, rank, most = call(
        functools.partial(place_body, peers=peers, rows=rows),
        [((1, rows), I32), ((1, rows), I32), ((AUX, LANES), F32)],
        [],
        (owner, slot),
        flops=2 * work,
    )
    f1, g1, up, down, inner = middle(f, up, down, inner)
    up, down = passed(up, down)
    mixes = (mix_in, mix_out_t, bias_in)
    packed = (2 * chans + PAD, rows)
    ended = call(
        functools.partial(first_end_body, **line, peers=peers, cap=cap, go=go, rows=rows),
        [(full, BF), (full, BF), (chunk, BF)] + [(packed, BF)] * several,
        [pltpu.VMEM(packed, BF)] * (not several) + [blocks, *pack_s],
        (
            cols, tiles, f, g, f1, g1, up, down, inner, pool, *mixes,
            dest, rank, most, slot, owner,
        ),
        smem=1,
        flops=4 * work,
        limit=32,
    )
    f2, g2, buffer = ended[:3]
    sent = ended[-1]
    got = exchanged(buffer)

    def unpacked(back, step):
        return call(
            functools.partial(unpack_body, **ways),
            [((2 * chans, rows), BF)],
            lift_s,
            (step, back, dest, rank),
            smem=1,
        )[0]

    def received(step):
        return exchanged(
            call(
                functools.partial(pack_body, **ways),
                [(chunk, BF)],
                pack_s,
                (step.reshape(1), sent, dest, rank, most),
                smem=1,
                limit=32,
            )[0]
        )

    def add(step, totals):
        return call(
            functools.partial(totals_body, **sizes),
            [((2 * chans, coarse_rows), F32)],
            [hot_s, masked_s],
            (received(step), totals),
            limit=32,
        )[0]

    if several:
        rounds = jnp.max(got[:, chans + 2, 0].astype(F32)).astype(I32)
        totals = lax.fori_loop(0, rounds, add, jnp.zeros((2 * chans, coarse_rows), F32))
        values, mid = call(
            math_body,
            [((2 * chans, coarse_rows), BF), ((2 * chans, chans), F32)],
            [],
            (totals, mid_w, mid_t, bias_mid),
        )

        def fetch(step, lifted):
            back = call(
                functools.partial(gather_body, **sizes),
                [(reply, BF)],
                [hot_s],
                (received(step), values),
                limit=32,
            )[0]
            return lifted + unpacked(exchanged(back), step.reshape(1))

        lifted = lax.fori_loop(0, rounds, fetch, jnp.zeros((2 * chans, rows), BF))
    else:
        back, mid = call(
            functools.partial(coarse_body, **sizes),
            [(reply, BF), ((2 * chans, chans), F32)],
            [hot_s, masked_s],
            (got, mid_w, mid_t, bias_mid),
            limit=32,
        )
        lifted = unpacked(exchanged(back), jnp.zeros((1,), I32))

    merged, pre_grad, up, down, inner = call(
        functools.partial(second_start_body, **line),
        [(full, BF), (full, BF), (halo, BF), (halo, BF), (full, F32)],
        [ext],
        (cols, tiles, lifted, f, f1, f2, g, g1, g2, pool, *mixes),
        smem=1,
        flops=work,
    )
    up, down = passed(up, down)
    local = call(
        functools.partial(weights_body, chans=chans, cap=cap),
        [((lax.axis_size("region"), 2 * chans, LANES), BF)],
        [],
        (merged, pre_grad, f, f1, f2, g, g1, g2, mid, most),
        flops=work,
    )[0]
    m1, p1, up, down, inner = middle(merged, up, down, inner)
    up, down = passed(up, down)
    result, input_grad = call(
        functools.partial(second_end_body, **line),
        [(full, BF), (full, BF)],
        [pltpu.VMEM(full, BF), pltpu.VMEM(full, BF), blocks],
        (
            cols, tiles, merged, pre_grad, m1, p1, up, down, inner,
            mix_out, mix_in_t,
        ),
        smem=1,
        flops=2 * work,
    )
    factor = 1.0 / math.sqrt(lax.axis_size("geo") * rows * peers)
    got = lax.all_to_all(local, "region", 0, 0, tiled=True)
    rest = lax.axis_size("geo") * lax.axis_size("sub")
    spread = call(relay_body, [((rest, 2 * chans, LANES), BF)], [], (got,))[0]
    got = lax.all_to_all(spread, ("geo", "sub"), 0, 0, tiled=True)
    sum_weights, sum_biases, over = call(
        functools.partial(last_body, chans=chans, factor=factor),
        [((7, chans, chans), F32), ((2, chans), F32), ((1,), F32)],
        [pltpu.VMEM((2 * chans, LANES), F32)],
        (got,),
        smem_out=(2,),
    )
    return result, input_grad, sum_weights, sum_biases, over.reshape(())


def solution(mesh):
    line = ("region", "sub")
    in_specs = (
        P("geo", None, line),
        P("geo", line, None, None, None),
        P("geo", line, None),
        P("geo", line, None),
        P("geo", line),
        P("geo", line),
        P(),
        P(),
        P(),
        P(),
        P("geo", None, line),
    )
    out_specs = (P("geo", None, line), P("geo", None, line), P(), P())
    return jax.shard_map(
        on_device, mesh=mesh, in_specs=in_specs, out_specs=out_specs, check_vma=False
    )
```

```python
import functools
import math

import jax
import jax.numpy as jnp
from jax import lax
from jax.experimental import pallas as pl
from jax.experimental.pallas import tpu as pltpu
from jax.sharding import PartitionSpec as P


LINE = ("region", "sub")
BF = jnp.bfloat16
F32 = jnp.float32
I32 = jnp.int32
LANES = 128
AUX = 8
START_LIMIT = 16
PAD = 16

VM = pl.BlockSpec(memory_space=pltpu.VMEM)
SM = pl.BlockSpec(memory_space=pltpu.SMEM)


def call(body, outs, scratch, args, smem=0, flops=0, limit=24, far=(), smem_out=()):
    specs = [SM] * smem + [VM] * (len(args) - smem)
    for i in far:
        specs[i] = pl.BlockSpec(memory_space=pl.ANY)
    moved = sum(a.size * a.dtype.itemsize for a in args)
    return pl.pallas_call(
        body,
        out_shape=tuple(jax.ShapeDtypeStruct(s, d) for s, d in outs),
        in_specs=specs,
        out_specs=tuple(SM if i in smem_out else VM for i in range(len(outs))),
        scratch_shapes=scratch,
        cost_estimate=pl.CostEstimate(flops=flops, bytes_accessed=moved, transcendentals=0),
        compiler_params=pltpu.CompilerParams(vmem_limit_bytes=limit << 20),
    )(*args)


def dot(a, b):
    return jnp.dot(a, b, preferred_element_type=F32)


def dot_nt(a, b):
    return lax.dot_general(a, b, (((1,), (1,)), ((), ())), preferred_element_type=F32)


def lanes(k):
    if isinstance(k, int):
        return slice(k * LANES, (k + 1) * LANES)
    return pl.ds(pl.multiple_of(k * LANES, LANES), LANES)


def tile(ref, k):
    return ref[:, lanes(k)]


def each(count, one, compact):
    if not compact:
        for k in range(count):
            one(k)
        return

    def body(k, carry):
        one(k)
        return carry

    lax.fori_loop(0, count, body, 0)


def shifted(value, by):
    peers = lax.axis_size(LINE)
    pairs = [(i, i + by) for i in range(peers) if 0 <= i + by < peers]
    return lax.ppermute(value, LINE, pairs)


def add_transposed(cols, tiles, grad_of, ext, count, nonzero, compact):
    ext[...] = jnp.zeros_like(ext)

    def one(k):
        y = dot_nt(grad_of(k), row_tiles(tiles, k, nonzero))
        for n in range(nonzero):
            ext[cols[n, k]] += y[:, n * LANES : (n + 1) * LANES]

    each(count, one, compact)


def row_tiles(tiles, k, nonzero):
    return tiles[pl.ds(k * nonzero, nonzero)].reshape(nonzero * LANES, LANES)


def row_product(cols, tiles, blocks, k, nonzero):
    picked = [blocks[cols[n, k]] for n in range(nonzero)]
    return dot(jnp.concatenate(picked, axis=1), row_tiles(tiles, k, nonzero))


def fill_blocks(blocks, field, up, down, chans, count, compact):
    blocks[0] = up[0:chans, :]
    blocks[count + 1] = down[0:chans, :]

    def one(k):
        blocks[k + 1] = tile(field, k)

    each(count, one, compact)


def write_sends(up, down, first, last, ext, chans, count):
    up[0:chans, :] = last
    up[chans : 2 * chans, :] = ext[count + 1].astype(BF)
    down[0:chans, :] = first
    down[chans : 2 * chans, :] = ext[0].astype(BF)


def inner_tile(inner, up, down, k, chans, count):
    value = tile(inner, k)
    if not isinstance(k, int):
        first = jnp.where(k == 0, 1.0, 0.0)
        last = jnp.where(k == count - 1, 1.0, 0.0)
        value = value + first * up[chans : 2 * chans, :].astype(F32)
        return value + last * down[chans : 2 * chans, :].astype(F32)
    if k == 0:
        value = value + up[chans : 2 * chans, :].astype(F32)
    if k == count - 1:
        value = value + down[chans : 2 * chans, :].astype(F32)
    return value


def start_body(
    cols, tiles_h, f_h, g_h, up, down, inner, tiles, ext, g, edges, sems,
    *, chans, count, nonzero, compact
):
    pieces = 4 if count % 4 == 0 else 1
    size = count // pieces
    ends = [slice(0, LANES), slice((count - 1) * LANES, count * LANES)]
    others = [pltpu.make_async_copy(g_h, g, sems.at[pieces])]
    for i, at in enumerate(ends):
        others.append(pltpu.make_async_copy(f_h.at[:, at], edges.at[i], sems.at[pieces + 1 + i]))
    for c in others:
        c.start()
    copies = []
    for i in range(pieces):
        at = slice(i * size * nonzero, (i + 1) * size * nonzero)
        copies.append(pltpu.make_async_copy(tiles_h.at[at], tiles.at[at], sems.at[i]))
        copies[-1].start()
    for c in others:
        c.wait()
    if compact:
        for c in copies:
            c.wait()

    def grad_of(k):
        if not compact and k % size == 0:
            copies[k // size].wait()
        return tile(g, k)

    add_transposed(cols, tiles, grad_of, ext, count, nonzero, compact)
    write_sends(up, down, edges[0], edges[1], ext, chans, count)

    def one(k):
        inner[:, lanes(k)] = ext[k + 1]

    each(count, one, compact)


def middle_body(
    cols, tiles, f, up, down, inner, f1, g1, up2, down2, inner2, blocks, ext,
    *, chans, count, nonzero, compact
):
    fill_blocks(blocks, f, up, down, chans, count, compact)

    def one(k):
        g1[:, lanes(k)] = inner_tile(inner, up, down, k, chans, count).astype(BF)

    each(count, one, compact)

    def one(k):
        f1[:, lanes(k)] = row_product(cols, tiles, blocks, k, nonzero).astype(BF)

    each(count, one, compact)
    add_transposed(cols, tiles, lambda k: tile(g1, k), ext, count, nonzero, compact)
    write_sends(up2, down2, tile(f1, 0), tile(f1, count - 1), ext, chans, count)

    def one(k):
        inner2[:, lanes(k)] = ext[k + 1]

    each(count, one, compact)


def second_terms(
    cols, tiles, f, g, f1, up, down, inner, blocks, f2, g2, chans, count, nonzero, compact
):
    fill_blocks(blocks, f1, up, down, chans, count, compact)

    def one(k):
        at = lanes(k)
        y = row_product(cols, tiles, blocks, k, nonzero)
        f2[:, at] = (2.0 * y - f[:, at].astype(F32)).astype(BF)
        z = inner_tile(inner, up, down, k, chans, count)
        g2[:, at] = (2.0 * z - g[:, at].astype(F32)).astype(BF)

    each(count, one, compact)


def prepare_body(
    w_in, w_mid, w_out, biases, mix_in, mix_in_t, mix_out, mix_out_t, mid, mid_t, bias_in, bias_mid,
    *, chans
):
    flip = lambda w: w.astype(F32).T.astype(BF)
    for source, plain, turned in ((w_in, mix_in, mix_in_t), (w_out, mix_out, mix_out_t)):
        plain[...] = jnp.concatenate([source[k] for k in range(3)], axis=1)
        turned[...] = jnp.concatenate([flip(source[k]) for k in range(3)], axis=1)
    mid[...] = w_mid[...]
    mid_t[...] = flip(w_mid[...])
    same = lax.broadcasted_iota(I32, (chans, chans), 0) == lax.broadcasted_iota(I32, (chans, chans), 1)
    for row, column in ((0, bias_in), (1, bias_mid)):
        column[...] = jnp.sum(jnp.where(same, biases[row : row + 1, :], 0.0), axis=1, keepdims=True)


def place_body(owner, slot, dest, rank, most, *, peers, rows):
    d = owner[...] + slot[...]
    d = d - (d // peers) * peers
    dest[...] = d
    hot = lax.broadcasted_iota(I32, (peers, rows), 0) == d
    hot = jnp.where(hot, 1.0, 0.0).astype(F32)
    a = lax.broadcasted_iota(I32, (LANES, LANES), 0)
    b = lax.broadcasted_iota(I32, (LANES, LANES), 1)
    before = jnp.where(a < b, 1.0, 0.0).astype(BF)
    carry = jnp.zeros((peers, 1), F32)
    for k in range(rows // LANES):
        h = hot[:, k * LANES : (k + 1) * LANES]
        c = dot(h.astype(BF), before) + carry
        rank[:, k * LANES : (k + 1) * LANES] = jnp.sum(h * c, axis=0, keepdims=True).astype(I32)
        carry = carry + jnp.sum(h, axis=1, keepdims=True)
    most[...] = jnp.broadcast_to(jnp.max(carry, axis=0, keepdims=True), (AUX, LANES))


def slot_hot(dest, rank, step, cap, go, rows):
    at = rank - step * cap
    inside = (at >= 0) & (at < cap)
    col = jnp.where(inside, (dest - (dest // go) * go) * cap + at, -1)
    hot = lax.broadcasted_iota(I32, (go * cap, rows), 0) == col
    return jnp.where(hot, 1.0, 0.0).astype(BF)


def merge_halves(low, high, odd, cap):
    if cap == LANES // 2:
        left = lax.broadcasted_iota(I32, low.shape, 1) < cap
        if odd:
            return jnp.where(left, pltpu.roll(low, cap, 1), high)
        return jnp.where(left, low, pltpu.roll(high, cap, 1))
    at = slice(cap, 2 * cap) if odd else slice(0, cap)
    return jnp.concatenate([low[:, at], high[:, at]], axis=1)


def pack_into(
    buffer, big, out, sent, dest, rank, most, step, *, chans, peers, cap, go, rows, compact
):
    unroll = 1 if compact else peers // go
    high = 2 * chans + PAD
    group = dest // go

    def mask(g, carry):
        here = jnp.where(group == g, 1.0, 0.0).astype(BF)
        big[pl.ds(pl.multiple_of(g * high, high), high), :] = sent[...] * here
        return carry

    lax.fori_loop(0, peers // go, mask, 0, unroll=unroll)
    out[...] = dot_nt(big[...], slot_hot(dest, rank, step, cap, go, rows))
    row = lax.broadcasted_iota(I32, (AUX, 2 * cap), 0)
    lane = lax.broadcasted_iota(I32, (AUX, 2 * cap), 1)
    extra = jnp.where((row == 1) & (lane >= cap), float(LANES), 0.0)
    extra = extra + jnp.where(row == 2, most, 0.0)

    def place(g, carry):
        part = out[pl.ds(pl.multiple_of(g * high, high), high), :]
        for o in range(go):
            pair = o // 2 * 2 * cap
            near = jnp.concatenate([part] * 2, axis=1) if go == 1 else part[:, pair : pair + 2 * cap]
            odd = o % 2 == 1
            p = g * go + o
            body = merge_halves(near[0:chans], near[chans : 2 * chans], odd, cap)
            buffer[p, 0:chans, :] = body.astype(BF)
            aux = near[2 * chans : 2 * chans + AUX]
            buffer[p, chans : chans + AUX, :] = (merge_halves(aux, aux, odd, cap) + extra).astype(BF)
        return carry

    lax.fori_loop(0, peers // go, place, 0, unroll=unroll)


def pack_body(step, sent, dest, rank, most, buffer, big, out, *, cap, **sizes):
    needed = jnp.ceil(most[0:1, 0:1] * (1.0 / cap))
    pack_into(buffer, big, out, sent, dest[...], rank[...], needed, step[0], cap=cap, **sizes)


def unpack_body(
    step, back, dest, rank, lifted, big, hot, *, chans, peers, cap, go, rows, compact
):
    unroll = 1 if compact else peers // go
    hot[...] = slot_hot(dest[...], rank[...], step[0], cap, go, rows)
    high = 2 * chans

    def gather(g, carry):
        rows_low = pl.ds(pl.multiple_of(g * high, high), chans)
        rows_top = pl.ds(pl.multiple_of(g * high + chans, chans), chans)
        for o in range(0, go, 2):
            a = back[g * go + o].astype(F32)
            if go == 1:
                low, top = a[:, 0:cap], a[:, cap : 2 * cap]
                at = slice(0, cap)
            else:
                b = back[g * go + o + 1].astype(F32)
                at = slice(o * cap, (o + 2) * cap)
                if cap == LANES // 2:
                    low, top = merge_halves(a, b, False, cap), merge_halves(a, b, True, cap)
                else:
                    low = jnp.concatenate([a[:, 0:cap], b[:, 0:cap]], axis=1)
                    top = jnp.concatenate([a[:, cap:], b[:, cap:]], axis=1)
            big[rows_low, at] = low.astype(BF)
            big[rows_top, at] = top.astype(BF)
        return carry

    lax.fori_loop(0, peers // go, gather, 0, unroll=unroll)
    width = min(256, rows)

    def select(w, carry):
        at = pl.ds(pl.multiple_of(w * width, width), width)
        y = dot(big[...], hot[:, at])
        group = dest[:, at] // go
        total = jnp.zeros((high, width), F32)
        for g in range(peers // go):
            total = jnp.where(group == g, y[g * high : (g + 1) * high], total)
        lifted[:, at] = total.astype(BF)
        return carry

    lax.fori_loop(0, rows // width, select, 0, unroll=1 if compact else rows // width)


def coarse_hot(got, hot, masked, *, chans, peers, cap, parts, compact):
    wide = 2 * cap

    def one(p, carry):
        aux = got[p, chans : chans + AUX, :].astype(F32)
        at = pl.ds(pl.multiple_of(p * wide, wide), wide)
        code = aux[1:2, :].astype(I32)
        q = lax.broadcasted_iota(I32, (2 * LANES, wide), 0)
        hot[:, at] = jnp.where(q == code, 1.0, 0.0).astype(BF)
        if masked is not None:
            body = got[p, 0:chans, :].astype(F32)
            for h in range(parts):
                masked[h * chans : (h + 1) * chans, at] = jnp.where(
                    aux[0:1, :] == h + 1.0, body, 0.0
                ).astype(BF)
        return carry

    lax.fori_loop(0, peers, one, 0, unroll=4 if compact else 16)


def coarse_totals(hot, masked, chans, parts):
    acc = dot_nt(hot[...], masked[...]).T
    split = [acc[h * chans : (h + 1) * chans] for h in range(parts)]
    low = jnp.concatenate([s[:, 0:LANES] for s in split], axis=1)
    top = jnp.concatenate([s[:, LANES:] for s in split], axis=1)
    return low, top


def slope(value):
    sig = jax.nn.sigmoid(value)
    return sig * (1.0 + value * (1.0 - sig))


def coarse_math(coarse_sum, coarse_grad, weight, weight_t, bias, grads):
    coarse = coarse_sum.astype(BF)
    pre = dot(weight[...], coarse) + bias[...]
    out = (pre * jax.nn.sigmoid(pre)).astype(BF)
    mid_grad = (coarse_grad * slope(pre)).astype(BF)
    chans = pre.shape[0]
    grads[0:chans, :] = dot_nt(mid_grad, coarse)
    ones = jnp.ones((chans, mid_grad.shape[1]), BF)
    grads[chans : 2 * chans, :] = dot_nt(ones, mid_grad)
    return out, dot(weight_t[...], mid_grad).astype(BF)


def coarse_gather(back, got, hot, out, behind, *, chans, peers, cap, parts, compact):
    wide = 2 * cap
    stacked = [
        jnp.concatenate(
            [out[:, h * LANES : (h + 1) * LANES], behind[:, h * LANES : (h + 1) * LANES]], axis=1
        )
        for h in range(parts)
    ]
    stacked = jnp.concatenate(stacked, axis=0)
    step = max(1, 512 // wide)

    def one(b, carry):
        at = pl.ds(pl.multiple_of(b * step * wide, step * wide), step * wide)
        y = dot(stacked, hot[:, at])
        for j in range(step):
            p = b * step + j
            part = got[p, chans : chans + AUX, :].astype(F32)[0:1, :]
            total = jnp.zeros((chans, wide), F32)
            for h in range(parts):
                total = jnp.where(
                    part == h + 1.0,
                    y[h * chans : (h + 1) * chans, j * wide : (j + 1) * wide],
                    total,
                )
            back[p] = total.astype(BF)
        return carry

    lax.fori_loop(0, peers // step, one, 0, unroll=1 if compact else peers // step)


def coarse_body(got, weight, weight_t, bias, back, grads, hot, masked, **sizes):
    coarse_hot(got, hot, masked, **sizes)
    low, top = coarse_totals(hot, masked, sizes["chans"], sizes["parts"])
    out, behind = coarse_math(low, top, weight, weight_t, bias, grads)
    coarse_gather(back, got, hot, out, behind, **sizes)


def totals_body(got, before, after, hot, masked, **sizes):
    chans = sizes["chans"]
    coarse_hot(got, hot, masked, **sizes)
    low, top = coarse_totals(hot, masked, chans, sizes["parts"])
    after[0:chans, :] = before[0:chans, :] + low
    after[chans : 2 * chans, :] = before[chans : 2 * chans, :] + top


def math_body(totals, weight, weight_t, bias, values, grads):
    chans = totals.shape[0] // 2
    out, behind = coarse_math(
        totals[0:chans, :], totals[chans : 2 * chans, :], weight, weight_t, bias, grads
    )
    values[0:chans, :] = out
    values[chans : 2 * chans, :] = behind


def gather_body(got, values, back, hot, **sizes):
    chans = sizes["chans"]
    coarse_hot(got, hot, None, **sizes)
    coarse_gather(
        back, got, hot, values[0:chans, :], values[chans : 2 * chans, :], **sizes
    )


def mixed(mix, first, second, third, k):
    at = lanes(k)
    return dot(mix[...], jnp.concatenate([first[:, at], second[:, at], third[:, at]], axis=0))


def first_end_body(
    cols, tiles, f, g, f1, g1, up, down, inner, pool, mix_in, mix_out_t, bias,
    dest, rank, most, slot, owner,
    f2, g2, buffer, sent, blocks, big, out,
    *, chans, count, nonzero, compact, peers, cap, go, rows
):
    second_terms(
        cols, tiles, f, g, f1, up, down, inner, blocks, f2, g2, chans, count, nonzero, compact
    )

    def one(k):
        at = lanes(k)
        w = pool[:, at]
        pre = mixed(mix_in, f, f1, f2, k) + bias[...]
        h = (pre * jax.nn.sigmoid(pre)).astype(BF)
        m = mixed(mix_out_t, g, g1, g2, k).astype(BF)
        sent[0:chans, at] = (w * h.astype(F32)).astype(BF)
        sent[chans : 2 * chans, at] = (w * m.astype(F32)).astype(BF)

    each(count, one, compact)
    share = rows // 4 // peers
    index = owner[...] * share + slot[...] // peers
    part = index // LANES
    row = lax.broadcasted_iota(I32, (PAD, rows), 0)
    sent[2 * chans : 2 * chans + PAD, :] = (
        jnp.where(row == 0, part + 1, jnp.where(row == 1, index - part * LANES, 0))
        .astype(F32)
        .astype(BF)
    )
    needed = jnp.ceil(most[0:1, 0:1] * (1.0 / cap))
    pack_into(
        buffer, big, out, sent, dest[...], rank[...], needed, 0,
        chans=chans, peers=peers, cap=cap, go=go, rows=rows, compact=compact,
    )


def second_start_body(
    cols, tiles, lifted, f, f1, f2, g, g1, g2, pool, mix_in, mix_out_t, bias,
    merged, pre_grad, up, down, inner, ext,
    *, chans, count, nonzero, compact
):
    def fine(k):
        at = lanes(k)
        w = pool[:, at]
        pre = mixed(mix_in, f, f1, f2, k) + bias[...]
        sig = jax.nn.sigmoid(pre)
        h = (pre * sig).astype(BF)
        m = mixed(mix_out_t, g, g1, g2, k).astype(BF)
        merged[:, at] = (h.astype(F32) + w * lifted[0:chans, at].astype(F32)).astype(BF)
        hidden_grad = m.astype(F32) + w * lifted[chans : 2 * chans, at].astype(F32)
        pre_grad[:, at] = (hidden_grad * (sig * (1.0 + pre * (1.0 - sig)))).astype(BF)

    each(count, fine, compact)
    add_transposed(cols, tiles, lambda k: tile(pre_grad, k), ext, count, nonzero, compact)
    write_sends(up, down, tile(merged, 0), tile(merged, count - 1), ext, chans, count)

    def one(k):
        inner[:, lanes(k)] = ext[k + 1]

    each(count, one, compact)


def joined_body(
    cols, tiles, back, dest, rank, f, f1, f2, g, g1, g2, pool, mix_in, mix_out_t, bias,
    merged, pre_grad, up, down, inner, ext, lifted, big, hot,
    *, chans, count, nonzero, compact, peers, cap, go, rows
):
    unpack_body(
        (0,), back, dest, rank, lifted, big, hot,
        chans=chans, peers=peers, cap=cap, go=go, rows=rows, compact=compact,
    )
    second_start_body(
        cols, tiles, lifted, f, f1, f2, g, g1, g2, pool, mix_in, mix_out_t, bias,
        merged, pre_grad, up, down, inner, ext,
        chans=chans, count=count, nonzero=nonzero, compact=compact,
    )


def weights_body(merged, pre_grad, f, f1, f2, g, g1, g2, mid, most, local, *, chans, cap):
    p, m = pre_grad[...], merged[...]
    gin = [dot_nt(p, t[...]) for t in (f, f1, f2)]
    gout = [dot_nt(t[...], m) for t in (g, g1, g2)]
    total = dot_nt(jnp.ones(p.shape, BF), p)
    row = lax.broadcasted_iota(I32, (chans, chans), 0)
    sums = jnp.where(row == 0, total, mid[chans : 2 * chans, :])
    over = jnp.where(most[0:1, 0:1] > cap, 1.0, 0.0)
    sums = jnp.where(row == 2, over, sums)
    upper = jnp.concatenate(gin + [mid[0:chans, :]], axis=1).astype(BF)
    lower = jnp.concatenate(gout + [sums], axis=1).astype(BF)
    for i in range(local.shape[0]):
        local[i, 0:chans, :] = upper
        local[i, chans : 2 * chans, :] = lower


def second_end_body(
    cols, tiles, f, g, f1, g1, up, down, inner, mix_out, mix_in_t,
    result, input_grad, f2, g2, blocks,
    *, chans, count, nonzero, compact
):
    second_terms(
        cols, tiles, f, g, f1, up, down, inner, blocks, f2, g2, chans, count, nonzero, compact
    )

    def one(k):
        at = lanes(k)
        terms = jnp.concatenate([f[:, at], f1[:, at], f2[:, at]], axis=0)
        result[:, at] = dot(mix_out[...], terms).astype(BF)
        terms = jnp.concatenate([g[:, at], g1[:, at], g2[:, at]], axis=0)
        input_grad[:, at] = dot(mix_in_t[...], terms).astype(BF)

    each(count, one, compact)


def total_of(got):
    total = got[0].astype(F32)
    for i in range(1, got.shape[0]):
        total = total + got[i].astype(F32)
    return total


def relay_body(got, spread):
    total = total_of(got).astype(BF)
    for i in range(spread.shape[0]):
        spread[i] = total


def last_body(got, weights, biases, over, total, *, chans, factor):
    total[...] = total_of(got)
    over[0] = jnp.sum(total[chans + 2 : chans + 3, 3 * chans : 3 * chans + 1])
    for k in range(7):
        low = k // 4 * chans
        at = slice(k % 4 * chans, (k % 4 + 1) * chans)
        weights[k] = total[low : low + chans, at] * factor
    biases[...] = total[chans : chans + 2, 3 * chans : 4 * chans] * factor


def exchanged(buffer):
    return lax.all_to_all(buffer, LINE, 0, 0, tiled=True)


def on_device(*arrays):
    result, input_grad, weights, biases, over = level(*arrays, several=False)

    def again(carry):
        return (*level(*arrays, several=True)[:4], jnp.zeros_like(over))

    done = lax.while_loop(
        lambda carry: carry[4] > 0.5, again, (result, input_grad, weights, biases, over)
    )
    return done[0][None], done[1][None], done[2], done[3]


def level(
    features,
    lap_tiles,
    tile_cols,
    coarse_owner,
    coarse_slot,
    pool_weight,
    weight_in,
    weight_mid,
    weight_out,
    biases,
    out_grad,
    *,
    several,
):
    chans, rows = features.shape[1:]
    count, nonzero = lap_tiles.shape[1:3]
    peers = lax.axis_size(LINE)
    cap = 2 * rows // peers
    go = max(1, 256 // cap)
    coarse_rows = rows // 4
    parts = coarse_rows // LANES
    f, g = features[0], out_grad[0]
    tiles = lap_tiles[0].reshape(count * nonzero, LANES, LANES)
    cols = tile_cols[0].T
    owner = coarse_owner[0].reshape(1, rows)
    slot = coarse_slot
    pool = pool_weight
    line = dict(chans=chans, count=count, nonzero=nonzero, compact=several)
    ways = dict(chans=chans, peers=peers, cap=cap, go=go, rows=rows, compact=several)
    sizes = dict(chans=chans, peers=peers, cap=cap, parts=parts, compact=several)
    full = (chans, rows)
    halo = (2 * chans, LANES)
    ext = pltpu.VMEM((count + 2, chans, LANES), F32)
    blocks = pltpu.VMEM((count + 2, chans, LANES), BF)
    work = 2 * chans * rows * nonzero * LANES
    chunk = (peers, chans + AUX, 2 * cap)
    reply = (peers, chans, 2 * cap)
    hot_s = pltpu.VMEM((2 * LANES, peers * 2 * cap), BF)
    masked_s = pltpu.VMEM((parts * chans, peers * 2 * cap), BF)
    tall = peers // go * (2 * chans + PAD)
    pack_s = [pltpu.VMEM((tall, rows), BF), pltpu.VMEM((tall, go * cap), F32)]
    lift_s = [
        pltpu.VMEM((peers // go * 2 * chans, go * cap), BF),
        pltpu.VMEM((go * cap, rows), BF),
    ]
    small = (chans, chans)
    wide = (chans, 3 * chans)
    mix_in, mix_in_t, mix_out, mix_out_t, mid_w, mid_t, bias_in, bias_mid = call(
        functools.partial(prepare_body, chans=chans),
        [(wide, BF)] * 4 + [(small, BF)] * 2 + [((chans, 1), F32)] * 2,
        [],
        (weight_in, weight_mid, weight_out, biases),
        flops=2 * work,
    )

    def passed(up, down):
        up = shifted(up, 1)
        down = shifted(down, -1)
        return up, down

    def middle(field, up, down, inner):
        return call(
            functools.partial(middle_body, **line),
            [(full, BF), (full, BF), (halo, BF), (halo, BF), (full, F32)],
            [blocks, ext],
            (cols, tiles, field, up, down, inner),
            smem=1,
            flops=2 * work,
        )

    up, down, inner, tiles = call(
        functools.partial(start_body, **line),
        [(halo, BF), (halo, BF), (full, F32), (tiles.shape, BF)],
        [
            ext,
            pltpu.VMEM(full, BF),
            pltpu.VMEM((2, chans, LANES), BF),
            pltpu.SemaphoreType.DMA((7,)),
        ],
        (cols, tiles, f, g),
        smem=1,
        far=(1, 2, 3),
        limit=START_LIMIT,
        flops=work,
    )
    up, down = passed(up, down)
    dest, rank, most = call(
        functools.partial(place_body, peers=peers, rows=rows),
        [((1, rows), I32), ((1, rows), I32), ((AUX, LANES), F32)],
        [],
        (owner, slot),
        flops=2 * work,
    )
    f1, g1, up, down, inner = middle(f, up, down, inner)
    up, down = passed(up, down)
    mixes = (mix_in, mix_out_t, bias_in)
    packed = (2 * chans + PAD, rows)
    ended = call(
        functools.partial(first_end_body, **line, peers=peers, cap=cap, go=go, rows=rows),
        [(full, BF), (full, BF), (chunk, BF)] + [(packed, BF)] * several,
        [pltpu.VMEM(packed, BF)] * (not several) + [blocks, *pack_s],
        (
            cols, tiles, f, g, f1, g1, up, down, inner, pool, *mixes,
            dest, rank, most, slot, owner,
        ),
        smem=1,
        flops=4 * work,
        limit=32,
    )
    f2, g2, buffer = ended[:3]
    sent = ended[-1]
    got = exchanged(buffer)

    def unpacked(back, step):
        return call(
            functools.partial(unpack_body, **ways),
            [((2 * chans, rows), BF)],
            lift_s,
            (step, back, dest, rank),
            smem=1,
        )[0]

    def received(step):
        return exchanged(
            call(
                functools.partial(pack_body, **ways),
                [(chunk, BF)],
                pack_s,
                (step.reshape(1), sent, dest, rank, most),
                smem=1,
                limit=32,
            )[0]
        )

    def add(step, totals):
        return call(
            functools.partial(totals_body, **sizes),
            [((2 * chans, coarse_rows), F32)],
            [hot_s, masked_s],
            (received(step), totals),
            limit=32,
        )[0]

    if several:
        rounds = jnp.max(got[:, chans + 2, 0].astype(F32)).astype(I32)
        totals = lax.fori_loop(0, rounds, add, jnp.zeros((2 * chans, coarse_rows), F32))
        values, mid = call(
            math_body,
            [((2 * chans, coarse_rows), BF), ((2 * chans, chans), F32)],
            [],
            (totals, mid_w, mid_t, bias_mid),
        )

        def fetch(step, lifted):
            back = call(
                functools.partial(gather_body, **sizes),
                [(reply, BF)],
                [hot_s],
                (received(step), values),
                limit=32,
            )[0]
            return lifted + unpacked(exchanged(back), step.reshape(1))

        lifted = lax.fori_loop(0, rounds, fetch, jnp.zeros((2 * chans, rows), BF))
    else:
        back, mid = call(
            functools.partial(coarse_body, **sizes),
            [(reply, BF), ((2 * chans, chans), F32)],
            [hot_s, masked_s],
            (got, mid_w, mid_t, bias_mid),
            limit=32,
        )
        back = exchanged(back)

    body, first, extra = functools.partial(second_start_body, **line), [], []
    if several:
        first = [lifted]
    else:
        body = functools.partial(joined_body, **line, peers=peers, cap=cap, go=go, rows=rows)
        first = [back, dest, rank]
        extra = [pltpu.VMEM((2 * chans, rows), BF), *lift_s]
    merged, pre_grad, up, down, inner = call(
        body,
        [(full, BF), (full, BF), (halo, BF), (halo, BF), (full, F32)],
        [ext, *extra],
        (cols, tiles, *first, f, f1, f2, g, g1, g2, pool, *mixes),
        smem=1,
        flops=work,
    )
    up, down = passed(up, down)
    local = call(
        functools.partial(weights_body, chans=chans, cap=cap),
        [((lax.axis_size("region"), 2 * chans, LANES), BF)],
        [],
        (merged, pre_grad, f, f1, f2, g, g1, g2, mid, most),
        flops=work,
    )[0]
    m1, p1, up, down, inner = middle(merged, up, down, inner)
    up, down = passed(up, down)
    result, input_grad = call(
        functools.partial(second_end_body, **line),
        [(full, BF), (full, BF)],
        [pltpu.VMEM(full, BF), pltpu.VMEM(full, BF), blocks],
        (
            cols, tiles, merged, pre_grad, m1, p1, up, down, inner,
            mix_out, mix_in_t,
        ),
        smem=1,
        flops=2 * work,
    )
    factor = 1.0 / math.sqrt(lax.axis_size("geo") * rows * peers)
    got = lax.all_to_all(local, "region", 0, 0, tiled=True)
    rest = lax.axis_size("geo") * lax.axis_size("sub")
    spread = call(relay_body, [((rest, 2 * chans, LANES), BF)], [], (got,))[0]
    got = lax.all_to_all(spread, ("geo", "sub"), 0, 0, tiled=True)
    sum_weights, sum_biases, over = call(
        functools.partial(last_body, chans=chans, factor=factor),
        [((7, chans, chans), F32), ((2, chans), F32), ((1,), F32)],
        [pltpu.VMEM((2 * chans, LANES), F32)],
        (got,),
        smem_out=(2,),
    )
    return result, input_grad, sum_weights, sum_biases, over.reshape(())


def solution(mesh):
    line = ("region", "sub")
    in_specs = (
        P("geo", None, line),
        P("geo", line, None, None, None),
        P("geo", line, None),
        P("geo", line, None),
        P("geo", line),
        P("geo", line),
        P(),
        P(),
        P(),
        P(),
        P("geo", None, line),
    )
    out_specs = (P("geo", None, line), P("geo", None, line), P(), P())
    return jax.shard_map(
        on_device, mesh=mesh, in_specs=in_specs, out_specs=out_specs, check_vma=False
    )
```
